256 devices in a mesh: ctx: 16 (over z, core), exp: 16 (over x, y).
Axes of the slice: x: 4, y: 4, z: 8, core: 2. Of those that a mesh axis runs over, the one named last changes fastest.
Arguments:
- inner_input: bfloat16 [8192, 8192], P('ctx', 'exp'), may hold values from -6 to 6
- gate_input: bfloat16 [8192, 8192], P('ctx', 'exp'), may hold values from -6 to 6
- coupling_input: bfloat16 [8192, 256], P('ctx'), may hold values from -6 to 6
- step_input: float32 [8192, 128], P('ctx', 'exp'), may hold values from -7 to 140
- conv_inner: float32 [4, 8192], P(None, 'exp'), may hold values from -3 to 3
- conv_coupling: float32 [4, 256], replicated, may hold values from -3 to 3
- decay_log: float32 [128], P('exp'), may hold values from -5.3 to -2.5
- skip_gain: float32 [128], P('exp'), may hold values from 0.5 to 2
- norm_gain: float32 [8192], P('exp'), may hold values from 0.1 to 1.9
- out_weight: bfloat16 [8192, 4096], P('exp'), may hold values from -0.0625 to 0.0625
- residual: bfloat16 [8192, 4096], P(('ctx', 'exp')), may hold values from -6 to 6
- moe_gain: float32 [4096], replicated, may hold values from 0.1 to 1.9
- router_weight: bfloat16 [4096, 72], replicated, may hold values from -0.1875 to 0.1875
- routes: int32 [8192, 10], P(('ctx', 'exp')), may hold values from 0 to 71, all different within a row
- priority: int32 [256, 32], P(('ctx', 'exp')), may hold values from 0 to 31, each once within a row
- expert_in: bfloat16 [16, 4096, 1536], P('exp', 'ctx'), may hold values from -0.09375 to 0.09375
- expert_out: bfloat16 [16, 4096, 768], P('exp', 'ctx'), may hold values from -0.21875 to 0.21875
Outputs:
- hidden: float32 [8192, 4096], P(('ctx', 'exp'))
- moe_out: float32 [8192, 4096], P(('ctx', 'exp'))
The draws below stay inside these ranges and needn't reach their ends.
Inputs may be any that keep to these rules, and one draw needn't show every extreme that they name: `routes`: each token names 10 different experts. `priority`: the 32 tokens of each row carry distinct priorities.
All inputs are finite; a program needn't handle non-finite values.
Results may differ from the reference program's by a relative error of at most 0.029.
Values may be sent and summed in bfloat16 or wider, within the bound.
A program may use at most 128 MiB of HBM per device.

```python
import math
import jax
import jax.numpy as jnp
from jax import lax

D = 4096
MIXER_HEADS = 128
HDIM = 64
STATE = 128
KCONV = 4
NEXP = 72
TOPK = 10
FFE = 768
SPAN = 256
INNER = 8192
SEQUENCE_TOKENS = 8192
TOK_DEV = 32
FLIGHT = 16
CAP = 8
N_CTX = 16
N_EXP = 16


def head_rates(key):
    share = 0.5
    rapid_decay = jax.random.bernoulli(jax.random.fold_in(key, 11), share, (MIXER_HEADS,))
    slow_log = jax.random.uniform(jax.random.fold_in(key, 12), (MIXER_HEADS,), jnp.float32, math.log(0.005), math.log(0.02))
    fast_log = jax.random.uniform(jax.random.fold_in(key, 13), (MIXER_HEADS,), jnp.float32, math.log(0.03), math.log(0.08))
    return (rapid_decay, jnp.where(rapid_decay, fast_log, slow_log))


def draw_decay_log(key, part):
    return head_rates(key)[1]


def draw_step_input(key, part):
    rapid_decay, decay = head_rates(key)
    brisk_rate = jax.random.uniform(jax.random.fold_in(key, 21), (SEQUENCE_TOKENS, MIXER_HEADS), jnp.float32, -1.0, 0.5)
    gentle_decay = jax.random.uniform(jax.random.fold_in(key, 22), (SEQUENCE_TOKENS, MIXER_HEADS), jnp.float32, -7.0, -5.6)
    sudden_spike = jax.random.bernoulli(jax.random.fold_in(key, 23), 2.0 / SEQUENCE_TOKENS, (SEQUENCE_TOKENS, MIXER_HEADS))
    loss = jax.random.uniform(jax.random.fold_in(key, 24), (SEQUENCE_TOKENS, MIXER_HEADS), jnp.float32, 0.22, 0.69)
    sudden_leap = loss / jnp.exp(decay)[None, :]
    return jnp.where(sudden_spike, sudden_leap, jnp.where(rapid_decay[None, :], brisk_rate, gentle_decay))


def levels(rng, dims, split, low, largest):
    def one(dim, blocks):
        steps = jax.random.uniform(jax.random.fold_in(jax.random.fold_in(rng, 6), dim), (blocks,), jnp.float32, low / len(split), largest / len(split))
        return jnp.repeat(jnp.exp(steps), dims[dim] // blocks).reshape((-1,) + (1,) * (len(dims) - dim - 1))

    factor_of = one(*split[0])
    for cut in split[1:]:
        factor_of = factor_of * one(*cut)
    return factor_of


def distinct(stream_key, rows, number_of, top, lift):
    ranking = jax.random.permutation(jax.random.fold_in(stream_key, 1), number_of)
    pull = ranking
    for power in range(3):
        pull = pull * pull // number_of
    pull = pull * lift // number_of
    tickets = jax.random.randint(jax.random.fold_in(stream_key, 2), (rows, number_of), 0, 4096) + pull
    fixed_rows = jax.random.permutation(jax.random.fold_in(stream_key, 3), rows)[jnp.arange(number_of) % rows]
    tickets = jnp.where(jnp.arange(rows)[:, None] == fixed_rows[None, :], 1 << 14, tickets)
    merit = tickets * number_of + jnp.arange(number_of)
    return lax.top_k(merit.astype(jnp.int32), top)[1].astype(jnp.int32)


def noise(rng, extent, scale, reach, split=(), held_as=jnp.bfloat16):
    drawn = scale * jax.random.normal(rng, extent, jnp.float32)
    if split:
        drawn = drawn * levels(rng, extent, split, -0.22, 0.18)
    return jnp.clip(drawn, -reach, reach).astype(held_as)


def setup_inputs(seed: int = 0) -> dict:
    streams_of = jax.random.split(jax.random.key(seed), 18)
    return {
        "inner_input": noise(streams_of[0], (SEQUENCE_TOKENS, INNER), 1.0, 6.0, ((0, 16), (1, 16))),
        "gate_input": noise(streams_of[1], (SEQUENCE_TOKENS, INNER), 1.0, 6.0, ((0, 16), (1, 16))),
        "coupling_input": noise(streams_of[2], (SEQUENCE_TOKENS, 2 * STATE), 1.0, 6.0, ((0, 16),)),
        "step_input": draw_step_input(jax.random.fold_in(streams_of[17], 71), 0),
        "conv_inner": noise(streams_of[4], (KCONV, INNER), KCONV ** -0.5, 3.0, ((1, 16),), jnp.float32),
        "conv_coupling": noise(streams_of[5], (KCONV, 2 * STATE), KCONV ** -0.5, 3.0, (), jnp.float32),
        "decay_log": draw_decay_log(jax.random.fold_in(streams_of[17], 71), 0),
        "skip_gain": jnp.clip(0.5 + 1.5 * jax.random.uniform(streams_of[7], (MIXER_HEADS,), jnp.float32) ** levels(streams_of[7], (MIXER_HEADS,), ((0, 16),), -0.2, 0.2), 0.5, 2.0),
        "norm_gain": jnp.clip(1.0 + 0.18 * jax.random.normal(streams_of[8], (INNER,), jnp.float32), 0.1, 1.9),
        "out_weight": noise(streams_of[9], (INNER, D), INNER ** -0.5, 0.0625, ((0, 16),)),
        "residual": noise(streams_of[10], (SEQUENCE_TOKENS, D), 1.0, 6.0, ((0, 256),)),
        "moe_gain": jnp.clip(1.0 + 0.18 * jax.random.normal(streams_of[11], (D,), jnp.float32), 0.1, 1.9),
        "router_weight": noise(streams_of[12], (D, NEXP), (D // 4) ** -0.5, 0.1875),
        "routes": distinct(streams_of[13], SEQUENCE_TOKENS, NEXP, TOPK, 2275),
        "priority": jax.vmap(lambda own: jax.random.permutation(own, TOK_DEV))(jax.random.split(streams_of[14], (N_CTX * N_EXP))).reshape((N_CTX * N_EXP, TOK_DEV)).astype(jnp.int32),
        "expert_in": noise(streams_of[15], (FLIGHT, D, 2 * FFE), D ** -0.5, 0.09375, ((0, 16), (1, 16))),
        "expert_out": noise(streams_of[16], (FLIGHT, D, FFE), FFE ** -0.5, 0.21875, ((0, 16), (1, 16))),
    }


EPS = 1e-05
HIGH = lax.Precision.HIGHEST

def causal_conv(values, weight):
    count = values.shape[0]
    padded = jnp.concatenate([jnp.zeros((KCONV - 1, values.shape[1]), jnp.float32), values.astype(jnp.float32)], axis=0)
    total = jnp.zeros((count, values.shape[1]), jnp.float32)
    for k in range(KCONV):
        total = total + weight[k][None, :] * padded[k:k + count]
    return jax.nn.silu(total).astype(jnp.bfloat16)

def block_terms(inner, inputs, outputs, steps, decay_log):
    rate = steps * (-jnp.exp(decay_log))[None, :]
    cums = jnp.cumsum(rate, axis=0)
    scores = jnp.dot(outputs, inputs.T, preferred_element_type=jnp.float32)
    above = (jnp.arange(SPAN)[:, None] >= jnp.arange(SPAN)[None, :])[None]
    flipped = cums.T
    spread = flipped[:, :, None] - flipped[:, None, :]
    decay = jnp.where(above, jnp.exp(jnp.where(above, spread, 0.0)), 0.0)
    mixing = (scores[None] * decay * steps.T[:, None, :]).astype(jnp.bfloat16)
    local = jnp.einsum('hij,jhp->ihp', mixing.astype(jnp.float32), inner.astype(jnp.float32), precision=HIGH)
    tail = jnp.exp(cums[-1][None, :] - cums) * steps
    state = jnp.einsum('jh,jn,jhp->hnp', tail, inputs.astype(jnp.float32), inner.astype(jnp.float32), precision=HIGH)
    return (local, jnp.exp(cums), state, jnp.exp(cums[-1]))

def reference(inner_input, gate_input, coupling_input, step_input, conv_inner, conv_coupling, decay_log, skip_gain, norm_gain, out_weight, residual, moe_gain, router_weight, routes, priority, expert_in, expert_out):
    inner = causal_conv(inner_input, conv_inner)
    coupling = causal_conv(coupling_input, conv_coupling)
    steps = jax.nn.softplus(step_input)
    blocks = SEQUENCE_TOKENS // SPAN
    inner_parts = inner.reshape(blocks, SPAN, MIXER_HEADS, HDIM)
    input_parts = coupling[:, :STATE].reshape(blocks, SPAN, STATE)
    output_parts = coupling[:, STATE:].reshape(blocks, SPAN, STATE)
    step_parts = steps.reshape(blocks, SPAN, MIXER_HEADS)

    def advance(carry, pieces):
        part_inner, part_in, part_out, part_steps = pieces
        local, growth, state, drop = block_terms(part_inner, part_in, part_out, part_steps, decay_log)
        carried = jnp.einsum('in,ih,hnp->ihp', part_out.astype(jnp.float32), growth, carry, precision=HIGH)
        result = local + carried + skip_gain[None, :, None] * part_inner.astype(jnp.float32)
        return (drop[:, None, None] * carry + state, result)
    start = jnp.zeros((MIXER_HEADS, STATE, HDIM), jnp.float32)
    _, results = lax.scan(advance, start, (inner_parts, input_parts, output_parts, step_parts))
    mixed = results.reshape(SEQUENCE_TOKENS, INNER)
    gated = mixed * jax.nn.silu(gate_input.astype(jnp.float32))
    squares = lax.optimization_barrier(jnp.sum(gated * gated, axis=1))
    scaled = (gated * norm_gain[None, :]).astype(jnp.bfloat16)
    group_cols = INNER // N_EXP
    scaled_groups = jnp.transpose(scaled.reshape(SEQUENCE_TOKENS, N_EXP, group_cols), (1, 0, 2))
    weight_groups = out_weight.reshape(N_EXP, group_cols, D)

    def head_group(total, pieces):
        columns, matrix = pieces
        term = jnp.dot(columns, matrix, preferred_element_type=jnp.float32).astype(jnp.bfloat16)
        return (total + lax.optimization_barrier(term).astype(jnp.float32), None)
    projected, _ = lax.scan(head_group, jnp.zeros((SEQUENCE_TOKENS, D), jnp.float32), (scaled_groups, weight_groups))
    mamba_out = projected * lax.rsqrt(squares / INNER + EPS)[:, None]
    hidden = residual.astype(jnp.float32) + mamba_out
    hidden_f = hidden
    normed = (hidden_f * lax.rsqrt(lax.optimization_barrier(jnp.mean(hidden_f * hidden_f, axis=1)) + EPS)[:, None] * moe_gain[None, :]).astype(jnp.bfloat16)
    logits = jnp.dot(normed, router_weight, preferred_element_type=jnp.float32)
    picked = jnp.take_along_axis(logits, routes, axis=1)
    raised = jnp.exp(picked)
    probs = raised / lax.optimization_barrier(jnp.sum(raised, axis=1, keepdims=True))
    match = routes[:, :, None] == jnp.arange(FLIGHT, dtype=jnp.int32)[None, None, :]
    member = lax.optimization_barrier(jnp.sum(match.astype(jnp.int32), axis=1))
    share = lax.optimization_barrier(jnp.sum(jnp.where(match, probs[:, :, None], 0.0), axis=1)).astype(jnp.bfloat16)
    groups = SEQUENCE_TOKENS // TOK_DEV
    member_groups = member.reshape(groups, TOK_DEV, FLIGHT)
    order = priority.reshape(groups, TOK_DEV)
    earlier = (order[:, None, :] < order[:, :, None]).astype(jnp.int32)
    rank = lax.optimization_barrier(jnp.sum(earlier[:, :, :, None] * member_groups[:, None, :, :], axis=2))
    kept = (member_groups > 0) & (rank < CAP)
    slots = kept[..., None] & (rank[..., None] == jnp.arange(CAP, dtype=jnp.int32)[None, None, None, :])
    select = jnp.transpose(slots, (2, 0, 3, 1)).astype(jnp.float32)
    share_groups = jnp.transpose(share.astype(jnp.float32).reshape(groups, TOK_DEV, FLIGHT), (2, 0, 1))
    weights = select * share_groups[:, :, None, :]
    normed_groups = normed.astype(jnp.float32).reshape(groups, TOK_DEV, D)
    slice_width = D // N_CTX

    def expert_step(total, pieces):
        first_matrix, second_matrix, pick, scale = pieces
        rows = jnp.einsum('bst,btd->bsd', pick, normed_groups).reshape(groups * CAP, D).astype(jnp.bfloat16)
        parts = jnp.einsum('rkw,kwf->krf', rows.astype(jnp.float32).reshape(groups * CAP, N_CTX, slice_width), first_matrix.astype(jnp.float32).reshape(N_CTX, slice_width, 2 * FFE), precision=HIGH).astype(jnp.bfloat16)
        units = lax.optimization_barrier(jnp.sum(lax.optimization_barrier(parts).astype(jnp.float32), axis=0))
        activated = (jax.nn.silu(units[:, :FFE]) * units[:, FFE:]).astype(jnp.bfloat16)
        answer = jnp.dot(activated, second_matrix.T, preferred_element_type=jnp.float32).astype(jnp.bfloat16)
        answer_groups = answer.astype(jnp.float32).reshape(groups, CAP, D)
        return (total + jnp.einsum('bst,bsd->btd', scale, answer_groups), None)
    total, _ = lax.scan(expert_step, jnp.zeros((groups, TOK_DEV, D), jnp.float32), (expert_in, expert_out, select, weights))
    moe_out = total.reshape(SEQUENCE_TOKENS, D)
    return (hidden, moe_out)
```

```python
import jax
import jax.numpy as jnp
from jax import lax
from jax.experimental import pallas as pl
from jax.experimental.pallas import tpu as pltpu
from jax.sharding import PartitionSpec as P

HDIM = 64
STATE = 128
KCONV = 4
NEXP = 72
TOPK = 10
FFE = 768
SPAN = 256
INNER = 8192
D = 4096
HEADS = 8
WIDTH = 512
COUNT = 512
TOK = 32
CAP = 8
FLIGHT = 16
SLICE = 256
RING = 8
CHUNKS = 4

EPS = 1e-05
HIGH = lax.Precision.HIGHEST
F32 = jnp.float32
BF16 = jnp.bfloat16
MESH = pl.DeviceIdType.MESH
VMEM_LIMIT = 56 * 1024 * 1024


def vmem():
    return pl.BlockSpec(memory_space=pltpu.VMEM)


def anyspace():
    return pl.BlockSpec(memory_space=pl.ANY)


def shaped(shape, dtype):
    return jax.ShapeDtypeStruct(shape, dtype)


def silu(x):
    return x * jax.nn.sigmoid(x)


def where_am_i():
    c = lax.axis_index("ctx")
    e = lax.axis_index("exp")
    return lax.div(c, 2), lax.rem(c, 2), lax.div(e, 4), lax.rem(e, 4)


def up_down(z, core):
    up = lax.rem(z + 1, RING) * 2 + core
    down = lax.rem(z + RING - 1, RING) * 2 + core
    return up, down


def remote(src, dst, send, recv, device):
    return pltpu.make_async_remote_copy(
        src_ref=src,
        dst_ref=dst,
        send_sem=send,
        recv_sem=recv,
        device_id=device,
        device_id_type=MESH,
    )


def conv_part(src_ref, halo, weight_ref, pad_ref):
    count = src_ref.shape[0]
    pad_ref[0:8, :] = halo.astype(F32)
    pad_ref[8 : 8 + count, :] = src_ref[...].astype(F32)
    total = weight_ref[0:1, :] * pad_ref[5 : 5 + count, :]
    for k in range(1, KCONV):
        total = total + weight_ref[k : k + 1, :] * pad_ref[5 + k : 5 + k + count, :]
    return silu(total).astype(BF16)


def expander():
    row = lax.broadcasted_iota(jnp.int32, (HEADS, WIDTH), 0)
    lane = lax.broadcasted_iota(jnp.int32, (HEADS, WIDTH), 1)
    return (lax.div(lane, HDIM) == row).astype(F32)


def spread_cols(values, expand):
    return lax.dot_general(
        values, expand, (((0,), (0,)), ((), ())), precision=HIGH, preferred_element_type=F32
    )


def spread_row(column, expand):
    return jnp.sum(column * expand, axis=0, keepdims=True)


def prepare_kernel(
    x_ref,
    cpl_ref,
    halo_ref,
    step_ref,
    cw_ref,
    cc_ref,
    decay_ref,
    inner_ref,
    coup_ref,
    steps_ref,
    cums_ref,
    first_ref,
    run_ref,
    reach_ref,
    drop_ref,
    pad_ref,
    padc_ref,
):
    inner_ref[...] = conv_part(x_ref, halo_ref[:, :WIDTH], cw_ref, pad_ref)
    coup_ref[...] = conv_part(cpl_ref, halo_ref[:, WIDTH:], cc_ref, padc_ref)
    raw = step_ref[...]
    steps = jnp.maximum(raw, 0.0) + jnp.log1p(jnp.exp(-jnp.abs(raw)))
    steps_ref[...] = steps
    rate = steps * (-jnp.exp(decay_ref[...]))
    row = lax.broadcasted_iota(jnp.int32, (SPAN, SPAN), 0)
    col = lax.broadcasted_iota(jnp.int32, (SPAN, SPAN), 1)
    upper = (row <= col).astype(F32)
    expand = expander()
    states = []
    drops = []
    for b in range(COUNT // SPAN):
        part = slice(b * SPAN, (b + 1) * SPAN)
        cums = jnp.dot(rate[:, part], upper, precision=HIGH, preferred_element_type=F32)
        cums_ref[:, part] = cums
        last = cums[:, SPAN - 1 : SPAN]
        tail = jnp.exp(last - cums) * steps[:, part]
        weighted = (inner_ref[part, :].astype(F32) * spread_cols(tail, expand)).astype(BF16)
        states.append(
            lax.dot_general(
                coup_ref[part, :STATE],
                weighted,
                (((0,), (0,)), ((), ())),
                preferred_element_type=F32,
            )
        )
        drops.append(spread_row(jnp.exp(last), expand))
    first_ref[...] = states[0]
    run_ref[...] = drops[1] * states[0] + states[1]
    reach_ref[...] = drops[0] * drops[1]
    drop_ref[...] = drops[0]


def mixer_kernel(
    inner_ref,
    coup_ref,
    steps_ref,
    cums_ref,
    first_ref,
    drop_ref,
    entry_ref,
    gate_ref,
    skip_ref,
    gain_ref,
    byx_ref,
    byy_ref,
    squares_ref,
    mixed_ref,
):
    expand = expander()
    row = lax.broadcasted_iota(jnp.int32, (SPAN, SPAN), 0)
    col = lax.broadcasted_iota(jnp.int32, (SPAN, SPAN), 1)
    above = row >= col
    lane = lax.broadcasted_iota(jnp.int32, (SPAN, 2 * HDIM), 1)
    for b in range(COUNT // SPAN):
        part = slice(b * SPAN, (b + 1) * SPAN)
        inputs = coup_ref[part, :STATE]
        outputs = coup_ref[part, STATE:]
        scores = lax.dot_general(
            outputs, inputs, (((1,), (1,)), ((), ())), preferred_element_type=F32
        )
        scores = jnp.where(above, scores, 0.0)
        cums = cums_ref[:, part]
        turned = cums.T
        entry = entry_ref[...]
        if b == 1:
            entry = drop_ref[...] * entry + first_ref[...]
        carried = jnp.dot(outputs, entry.astype(BF16), preferred_element_type=F32)
        carried = carried * spread_cols(jnp.exp(cums), expand)
        for pair in range(HEADS // 2):
            cols = slice(pair * 2 * HDIM, (pair + 1) * 2 * HDIM)
            values = inner_ref[part, cols]
            halves = []
            for h in (2 * pair, 2 * pair + 1):
                spread = turned[:, h : h + 1] - cums[h : h + 1, :]
                decay = jnp.exp(jnp.where(above, spread, 0.0))
                mixing = (scores * decay * steps_ref[h : h + 1, part]).astype(BF16)
                halves.append(jnp.dot(mixing, values, preferred_element_type=F32))
            local = jnp.where(lane < HDIM, halves[0], halves[1])
            mixed = local + carried[:, cols] + skip_ref[:, cols] * values.astype(F32)
            mixed_ref[part, cols] = mixed * silu(gate_ref[part, cols].astype(F32))
    gated = mixed_ref[...]
    squares_ref[...] = lax.dot_general(
        jnp.ones((8, WIDTH), F32),
        gated * gated,
        (((1,), (1,)), ((), ())),
        precision=HIGH,
        preferred_element_type=F32,
    )[0:1, :]
    scaled = (gated * gain_ref[...]).astype(BF16)
    byx_ref[...] = scaled
    for x in range(4):
        for y in range(4):
            byy_ref[(y * 4 + x) * TOK : (y * 4 + x + 1) * TOK, :] = scaled[
                (x * 4 + y) * TOK : (x * 4 + y + 1) * TOK, :
            ]


def chain_kernel(
    run_ref,
    reach_ref,
    wi_ref,
    entry_ref,
    iu1_ref,
    id1_ref,
    mine,
    theirs,
    their_reach,
    arriving,
    onward,
    hop_send,
    hop_recv,
    pair_send,
    pair_recv,
    chain_send,
    chain_recv,
    relay_send,
):
    z, core, _, _ = where_am_i()
    up, down = up_down(z, core)
    partner = z * 2 + 1 - core
    barrier = pltpu.get_barrier_semaphore()
    for other in (partner, up, down):
        pl.semaphore_signal(barrier, inc=1, device_id={"ctx": other}, device_id_type=MESH)
    pl.semaphore_wait(barrier, 3)

    hops = [
        remote(wi_ref, iu1_ref, hop_send.at[0], hop_recv.at[0], {"ctx": up}),
        remote(wi_ref, id1_ref, hop_send.at[1], hop_recv.at[1], {"ctx": down}),
    ]
    pairs = [
        remote(mine, theirs, pair_send.at[0], pair_recv.at[0], {"ctx": partner}),
        remote(reach_ref, their_reach, pair_send.at[1], pair_recv.at[1], {"ctx": partner}),
    ]
    rows = STATE // CHUNKS
    spans = [pl.ds(i * rows, rows) for i in range(CHUNKS)]
    ahead = [
        remote(onward.at[s], arriving.at[s], chain_send.at[i], chain_recv.at[i], {"ctx": up})
        for i, s in enumerate(spans)
    ]
    relays = [
        remote(arriving.at[s], arriving.at[s], relay_send.at[i], chain_recv.at[i], {"ctx": partner})
        for i, s in enumerate(spans)
    ]

    @pl.when(core == 0)
    def _():
        mine[...] = run_ref[...].astype(BF16)
        for copy in pairs:
            copy.start()
        for copy in hops:
            copy.start()

        @pl.when(z == 0)
        def _():
            entry_ref[...] = jnp.zeros_like(entry_ref)

        @pl.when(z > 0)
        def _():
            for i, s in enumerate(spans):
                relays[i].wait_recv()
                entry_ref[s, :] = arriving[s, :].astype(F32)

        for copy in pairs:
            copy.wait_send()

    @pl.when(core == 1)
    def _():
        for copy in hops:
            copy.start()
        for copy in pairs:
            copy.wait_recv()

        @pl.when(z == 0)
        def _():
            for i, s in enumerate(spans):
                before = theirs[s, :].astype(F32)
                onward[s, :] = (reach_ref[...] * before + run_ref[s, :]).astype(BF16)
                ahead[i].start()
                entry_ref[s, :] = before

        @pl.when(z > 0)
        def _():
            for i, s in enumerate(spans):
                before = theirs[s, :].astype(F32)
                ahead[i].wait_recv()
                inside = their_reach[...] * arriving[s, :].astype(F32) + before
                onward[s, :] = (reach_ref[...] * inside + run_ref[s, :]).astype(BF16)

                @pl.when(z < RING - 1)
                def _():
                    ahead[i].start()

                relays[i].start()
                entry_ref[s, :] = inside

            for copy in relays:
                copy.wait_send()

        @pl.when(z < RING - 1)
        def _():
            for copy in ahead:
                copy.wait_send()

    for copy in hops:
        copy.wait()


def project_kernel(
    byx_ref,
    byy_ref,
    w_ref,
    squares_ref,
    iu1_ref,
    id1_ref,
    owned_ref,
    sums_ref,
    iu2_ref,
    id2_ref,
    iu3_ref,
    id3_ref,
    parts,
    near,
    far,
    joined,
    near_sum,
    far_sum,
    all_squares,
    ring_send,
    ring_recv,
    sq_send,
    sq_recv,
    hop_send,
    hop_recv,
):
    z, core, x, y = where_am_i()
    up, down = up_down(z, core)
    me = x * 4 + y
    half = D // 2
    quarter = half // 2

    def peer(i):
        return lax.rem(me + i, FLIGHT)

    barrier = pltpu.get_barrier_semaphore()
    for other in (up, down):
        pl.semaphore_signal(barrier, inc=1, device_id={"ctx": other}, device_id_type=MESH)

    def greet(i, carry):
        pl.semaphore_signal(barrier, inc=1, device_id={"exp": peer(i)}, device_id_type=MESH)
        return carry

    lax.fori_loop(1, FLIGHT, greet, 0)
    pl.semaphore_wait(barrier, FLIGHT + 1)

    hops = [
        remote(iu1_ref, iu2_ref, hop_send.at[0], hop_recv.at[0], {"ctx": up}),
        remote(id1_ref, id2_ref, hop_send.at[1], hop_recv.at[1], {"ctx": down}),
        remote(iu2_ref, iu3_ref, hop_send.at[2], hop_recv.at[2], {"ctx": up}),
        remote(id2_ref, id3_ref, hop_send.at[3], hop_recv.at[3], {"ctx": down}),
    ]
    hops[0].start()
    hops[1].start()

    def squares_copy(i):
        return remote(
            squares_ref, all_squares.at[i], sq_send.at[i], sq_recv.at[i], {"exp": peer(i)}
        )

    def send_squares(i, carry):
        squares_copy(i).start()
        return carry

    lax.fori_loop(1, FLIGHT, send_squares, 0)

    def along_x(by):
        return {"exp": lax.rem(x + by, 4) * 4 + y}

    def along_y(by):
        return {"exp": x * 4 + lax.rem(y + by, 4)}

    low = pl.ds(0, quarter)
    high = pl.ds(quarter, quarter)

    def message(stage, side, number, src):
        slot = stage * 12 + side * 6 + number
        toward = along_x if side == stage else along_y
        landing = (near if stage == 0 else far).at[side, number]
        return remote(
            src,
            landing,
            ring_send.at[slot],
            ring_recv.at[slot],
            toward(1 if number % 2 == 0 else 3),
        )

    def block(stage, side, offset):
        if stage == 0:
            return parts.at[side, offset]
        place = y if side == 0 else x
        start = pl.multiple_of(lax.rem(place + offset, 4) * TOK, TOK)
        return joined.at[side, pl.ds(start, TOK)]

    def sources(stage, side):
        across = block(stage, side, 2)
        right = block(stage, side, 1)
        left = block(stage, side, 3)
        sums = near_sum if stage == 0 else far_sum
        return [
            across.at[:, low],
            across.at[:, high],
            right.at[:, high],
            left.at[:, low],
            sums.at[side, 0],
            sums.at[side, 1],
        ]

    copies = [
        [
            [message(stage, side, n, src) for n, src in enumerate(sources(stage, side))]
            for side in range(2)
        ]
        for stage in range(2)
    ]

    def multiply(side, offset):
        rows_ref = byx_ref if side == 0 else byy_ref
        place = x if side == 0 else y
        start = pl.multiple_of(lax.rem(place + offset, 4) * 128, 128)
        rows = rows_ref[pl.ds(start, 128), :]

        def one(i, carry):
            source = pl.ds(pl.multiple_of(side * half + i * 512, 512), 512)
            target = pl.ds(pl.multiple_of(i * 512, 512), 512)
            parts[side, offset, :, target] = jnp.dot(
                rows, w_ref[:, source], preferred_element_type=F32
            ).astype(BF16)
            return carry

        lax.fori_loop(0, half // 512, one, 0)

    def pass_on(stage, side):
        landing = near if stage == 0 else far
        sums = near_sum if stage == 0 else far_sum
        copies[stage][side][0].wait_recv()
        sums[side, 0] = (
            block(stage, side, 1)[:, low].astype(F32) + landing[side, 0].astype(F32)
        ).astype(BF16)
        copies[stage][side][4].start()
        copies[stage][side][1].wait_recv()
        sums[side, 1] = (
            block(stage, side, 3)[:, high].astype(F32) + landing[side, 1].astype(F32)
        ).astype(BF16)
        copies[stage][side][5].start()

    def collect(stage, side):
        landing = near if stage == 0 else far
        for n in (2, 3, 4, 5):
            copies[stage][side][n].wait_recv()
        own = block(stage, side, 0)
        first = own[:, low].astype(F32) + landing[side, 4].astype(F32)
        first = first + landing[side, 3].astype(F32)
        second = own[:, high].astype(F32) + landing[side, 2].astype(F32)
        second = second + landing[side, 5].astype(F32)
        return first, second

    for side in range(2):
        multiply(side, 2)
        copies[0][side][0].start()
        copies[0][side][1].start()
    for side in range(2):
        multiply(side, 1)
        copies[0][side][2].start()
        multiply(side, 3)
        copies[0][side][3].start()
    for side in range(2):
        pass_on(0, side)
    for side in range(2):
        multiply(side, 0)
    for side in range(2):
        first, second = collect(0, side)
        joined[side, :, low] = first.astype(BF16)
        joined[side, :, high] = second.astype(BF16)
        for n in range(4):
            copies[1][side][n].start()
    hops[0].wait_recv()
    hops[2].start()
    hops[1].wait_recv()
    hops[3].start()
    for side in range(2):
        pass_on(1, side)
    for side in range(2):
        first, second = collect(1, side)
        owned_ref[:, pl.ds(side * half, quarter)] = first
        owned_ref[:, pl.ds(side * half + quarter, quarter)] = second

    all_squares[0] = squares_ref[...]

    def take_squares(i, carry):
        squares_copy(i).wait()
        return carry

    lax.fori_loop(1, FLIGHT, take_squares, 0)
    total = all_squares[0]
    for i in range(1, FLIGHT):
        total = total + all_squares[i]
    sums_ref[...] = total

    for stage in range(2):
        for side in range(2):
            for copy in copies[stage][side]:
                copy.wait_send()
    hops[0].wait_send()
    hops[1].wait_send()
    hops[2].wait()
    hops[3].wait()


def route_kernel(
    owned_ref,
    sums_ref,
    residual_ref,
    gain_ref,
    router_ref,
    routes_ref,
    priority_ref,
    hidden_ref,
    rows_ref,
    weights_ref,
):
    me = lax.axis_index("exp")
    row = lax.broadcasted_iota(jnp.int32, (TOK, COUNT), 0)
    col = lax.broadcasted_iota(jnp.int32, (TOK, COUNT), 1)
    squares = jnp.sum(
        jnp.where(col == me * TOK + row, sums_ref[...], 0.0), axis=1, keepdims=True
    )
    hidden = residual_ref[...].astype(F32) + owned_ref[...] * lax.rsqrt(squares / INNER + EPS)
    hidden_ref[...] = hidden
    mean = jnp.sum(hidden * hidden, axis=1, keepdims=True) / D
    normed = (hidden * lax.rsqrt(mean + EPS) * gain_ref[...]).astype(BF16)
    logits = jnp.dot(normed, router_ref[...], preferred_element_type=F32)
    expert = lax.broadcasted_iota(jnp.int32, (TOK, NEXP), 1)
    named = expert < 0
    for k in range(TOPK):
        named = named | (routes_ref[:, k : k + 1] == expert)
    raised = jnp.where(named, jnp.exp(logits), 0.0)
    share = (raised / jnp.sum(raised, axis=1, keepdims=True)).astype(BF16)
    member = named.astype(F32).astype(BF16)
    square_row = lax.broadcasted_iota(jnp.int32, (TOK, TOK), 0)
    square_col = lax.broadcasted_iota(jnp.int32, (TOK, TOK), 1)
    order = priority_ref[...].astype(F32)
    own_order = jnp.sum(jnp.where(square_row == square_col, order, 0.0), axis=1, keepdims=True)
    earlier = (order < own_order).astype(F32).astype(BF16)
    rank = jnp.dot(earlier, member, preferred_element_type=F32)
    key = jnp.where(named, rank, 99.0).astype(BF16)
    lanes = FLIGHT * CAP
    wide_row = lax.broadcasted_iota(jnp.int32, (NEXP, lanes), 0)
    wide_col = lax.broadcasted_iota(jnp.int32, (NEXP, lanes), 1)
    widen = (lax.div(wide_col, CAP) == wide_row).astype(F32).astype(BF16)
    key_wide = jnp.dot(key, widen, preferred_element_type=F32)
    share_wide = jnp.dot(share, widen, preferred_element_type=F32)
    slot = lax.rem(lax.broadcasted_iota(jnp.int32, (TOK, lanes), 1), CAP).astype(F32)
    chosen = (key_wide == slot).astype(F32)
    weights_ref[...] = (chosen * share_wide).astype(BF16)
    pick = chosen.astype(BF16)
    for s in range(2 * RING):
        taken = lax.dot_general(
            pick,
            normed[:, s * SLICE : (s + 1) * SLICE],
            (((0,), (0,)), ((), ())),
            preferred_element_type=F32,
        )
        rows_ref[s % 2, :, :, (s // 2) * SLICE : (s // 2 + 1) * SLICE] = taken.reshape(
            FLIGHT, CAP, SLICE
        ).astype(BF16)


def expert_kernel(
    rows_ref,
    wi_ref,
    iu1_ref,
    id1_ref,
    iu2_ref,
    id2_ref,
    iu3_ref,
    id3_ref,
    wo_ref,
    back_ref,
    landed,
    tokens,
    weights,
    downs,
    units,
    units_out,
    units_in,
    answers,
    row_send,
    row_recv,
    back_send,
    back_recv,
    hop_send,
    hop_recv,
    load_sem,
    own_sem,
    pair_send,
    pair_recv,
):
    z, core, x, y = where_am_i()
    up, down = up_down(z, core)
    me = x * 4 + y
    partner = z * 2 + 1 - core
    plane = 2 * FLIGHT

    def peer(i):
        other = lax.rem(me + lax.div(i, 2), FLIGHT)
        other_core = lax.rem(core + i, 2)
        return other, other_core, {"ctx": z * 2 + other_core, "exp": other}

    barrier = pltpu.get_barrier_semaphore()
    for other in (up, down):
        pl.semaphore_signal(barrier, inc=1, device_id={"ctx": other}, device_id_type=MESH)

    def greet(i, carry):
        pl.semaphore_signal(barrier, inc=1, device_id=peer(i)[2], device_id_type=MESH)
        return carry

    lax.fori_loop(1, plane, greet, 0)
    pl.semaphore_wait(barrier, plane + 1)

    pieces = [wi_ref, iu1_ref, iu2_ref, iu3_ref, id1_ref, id2_ref, id3_ref]
    half = SLICE // 2
    hops = [
        remote(
            iu3_ref.at[pl.ds(0, half)],
            weights.at[7, pl.ds(0, half)],
            hop_send.at[0],
            hop_recv.at[0],
            {"ctx": up},
        ),
        remote(
            id3_ref.at[pl.ds(half, half)],
            weights.at[7, pl.ds(half, half)],
            hop_send.at[1],
            hop_recv.at[1],
            {"ctx": down},
        ),
    ]
    for n in range(3):
        src_up = wo_ref if n == 0 else downs.at[n]
        src_down = wo_ref if n == 0 else downs.at[3 + n]
        hops.append(
            remote(
                src_up, downs.at[n + 1], hop_send.at[2 * n + 2], hop_recv.at[2 * n + 2], {"ctx": up}
            )
        )
        hops.append(
            remote(
                src_down,
                downs.at[n + 4],
                hop_send.at[2 * n + 3],
                hop_recv.at[2 * n + 3],
                {"ctx": down},
            )
        )
    hops.append(
        remote(
            downs.at[3, pl.ds(0, half)],
            downs.at[7, pl.ds(0, half)],
            hop_send.at[8],
            hop_recv.at[8],
            {"ctx": up},
        )
    )
    hops.append(
        remote(
            downs.at[6, pl.ds(half, half)],
            downs.at[7, pl.ds(half, half)],
            hop_send.at[9],
            hop_recv.at[9],
            {"ctx": down},
        )
    )

    def row_copy(i):
        other, other_core, device = peer(i)
        return remote(
            rows_ref.at[other_core, other],
            landed.at[me, core],
            row_send.at[i],
            row_recv.at[i],
            device,
        )

    def start_rows(i, carry):
        row_copy(i).start()
        return carry

    lax.fori_loop(1, plane, start_rows, 0)
    for n in range(4):
        hops[n].start()
    own_rows = pltpu.make_async_copy(rows_ref.at[core, me], landed.at[me, core], own_sem.at[0])
    own_rows.start()
    loads = [
        pltpu.make_async_copy(piece, weights.at[n], load_sem.at[n]) for n, piece in enumerate(pieces)
    ]
    own_down = pltpu.make_async_copy(wo_ref, downs.at[0], own_sem.at[1])
    for copy in loads:
        copy.start()
    own_down.start()

    own_rows.wait()

    def take_rows(i, carry):
        row_copy(i).wait()
        return carry

    lax.fori_loop(1, plane, take_rows, 0)

    for s in range(RING):
        block = landed[:, :, :, s * SLICE : (s + 1) * SLICE].astype(F32)
        tokens[s] = block.reshape(plane * CAP, SLICE).astype(BF16)

    def source(n):
        if n <= 3:
            return lax.rem(z + RING - n, RING)
        if n <= 6:
            return lax.rem(z + n - 3, RING)
        return lax.rem(z + 4, RING)

    def forward(n):
        hops[n].wait_recv()
        hops[n + 2].start()

    for copy in loads:
        copy.wait()
    forward(2)
    forward(3)

    def gate_up(i, carry):
        cols = pl.ds(pl.multiple_of(i * 256, 256), 256)
        total = jnp.dot(tokens[source(0)], weights[0, :, cols], preferred_element_type=F32)
        for n in range(1, 7):
            total = total + jnp.dot(
                tokens[source(n)], weights[n, :, cols], preferred_element_type=F32
            )
        units[:, cols] = total
        return carry

    lax.fori_loop(0, 2 * FFE // 256, gate_up, 0)
    hops[0].wait_recv()
    hops[1].wait_recv()

    def last_slice(i, carry):
        cols = pl.ds(pl.multiple_of(i * 256, 256), 256)
        total = units[:, cols] + jnp.dot(
            tokens[source(7)], weights[7, :, cols], preferred_element_type=F32
        )
        units[:, cols] = total
        units_out[:, cols] = total.astype(BF16)
        return carry

    lax.fori_loop(0, 2 * FFE // 256, last_slice, 0)
    swap = remote(units_out, units_in, pair_send.at[0], pair_recv.at[0], {"ctx": partner})
    swap.start()
    swap.wait()
    gate = units[:, :FFE] + units_in[:, :FFE].astype(F32)
    lift = units[:, FFE:] + units_in[:, FFE:].astype(F32)
    activated = (silu(gate) * lift).astype(BF16)
    own_down.wait()

    def answer(n):
        values = lax.dot_general(
            activated, downs[n], (((1,), (1,)), ((), ())), preferred_element_type=F32
        )
        cols = pl.ds(pl.multiple_of(source(n) * SLICE, SLICE), SLICE)
        answers[:, :, :, cols] = values.reshape(FLIGHT, 2, CAP, SLICE).astype(BF16)

    answer(0)
    answer(1)
    answer(4)
    forward(4)
    forward(5)
    answer(2)
    answer(5)
    hops[6].wait_recv()
    hops[8].start()
    hops[7].wait_recv()
    hops[9].start()
    answer(3)
    answer(6)
    hops[8].wait_recv()
    hops[9].wait_recv()
    answer(7)

    def back_copy(i):
        other, other_core, device = peer(i)
        return remote(
            answers.at[other, other_core],
            back_ref.at[me, core],
            back_send.at[i],
            back_recv.at[i],
            device,
        )

    def start_back(i, carry):
        back_copy(i).start()
        return carry

    lax.fori_loop(1, plane, start_back, 0)
    own_back = pltpu.make_async_copy(answers.at[me, core], back_ref.at[me, core], own_sem.at[2])
    own_back.start()
    own_back.wait()

    def take_back(i, carry):
        back_copy(i).wait()
        return carry

    lax.fori_loop(1, plane, take_back, 0)
    for copy in hops:
        copy.wait_send()


def combine_kernel(weights_ref, back_ref, out_ref):
    weights = weights_ref[...]
    for j in range(2):
        rows = back_ref[:, j].astype(F32).reshape(FLIGHT * CAP, D // 2).astype(BF16)
        total = jnp.dot(weights, rows, preferred_element_type=F32)
        for s in range(RING):
            place = (2 * s + j) * SLICE
            out_ref[:, place : place + SLICE] = total[:, s * SLICE : (s + 1) * SLICE]


def call(kernel, outs, in_specs, out_specs, scratch=(), collective_id=None):
    if collective_id is None:
        params = pltpu.CompilerParams(vmem_limit_bytes=VMEM_LIMIT)
    else:
        params = pltpu.CompilerParams(
            vmem_limit_bytes=VMEM_LIMIT, collective_id=collective_id, has_side_effects=True
        )
    return pl.pallas_call(
        kernel,
        out_shape=outs,
        in_specs=in_specs,
        out_specs=out_specs,
        scratch_shapes=list(scratch),
        compiler_params=params,
    )


def body(
    inner_input,
    gate_input,
    coupling_input,
    step_input,
    conv_inner,
    conv_coupling,
    decay_log,
    skip_gain,
    norm_gain,
    out_weight,
    residual,
    moe_gain,
    router_weight,
    routes,
    priority,
    expert_in,
    expert_out,
):
    devices = lax.axis_size("ctx")
    edges = jnp.concatenate([inner_input[COUNT - 8 :], coupling_input[COUNT - 8 :]], axis=1)
    halo = lax.ppermute(edges, "ctx", [(i, i + 1) for i in range(devices - 1)])
    wi = expert_in[0]
    wo = expert_out[0]
    dma = pltpu.SemaphoreType.DMA

    inner, coup, steps, cums, first, run, reach, drop = call(
        prepare_kernel,
        (
            shaped((COUNT, WIDTH), BF16),
            shaped((COUNT, 2 * STATE), BF16),
            shaped((HEADS, COUNT), F32),
            shaped((HEADS, COUNT), F32),
            shaped((STATE, WIDTH), F32),
            shaped((STATE, WIDTH), F32),
            shaped((1, WIDTH), F32),
            shaped((1, WIDTH), F32),
        ),
        [vmem()] * 7,
        [vmem()] * 8,
        [pltpu.VMEM((COUNT + 8, WIDTH), F32), pltpu.VMEM((COUNT + 8, 2 * STATE), F32)],
    )(
        inner_input,
        coupling_input,
        halo,
        step_input.T,
        conv_inner,
        conv_coupling,
        decay_log[:, None],
    )

    piece = shaped((SLICE, 2 * FFE), BF16)
    entry, iu1, id1 = call(
        chain_kernel,
        (shaped((STATE, WIDTH), F32), piece, piece),
        [vmem(), vmem(), anyspace()],
        [vmem(), anyspace(), anyspace()],
        [
            pltpu.VMEM((STATE, WIDTH), BF16),
            pltpu.VMEM((STATE, WIDTH), BF16),
            pltpu.VMEM((1, WIDTH), F32),
            pltpu.VMEM((STATE, WIDTH), BF16),
            pltpu.VMEM((STATE, WIDTH), BF16),
            dma((2,)),
            dma((2,)),
            dma((2,)),
            dma((2,)),
            dma((CHUNKS,)),
            dma((CHUNKS,)),
            dma((CHUNKS,)),
        ],
        collective_id=0,
    )(run, reach, wi)

    byx, byy, squares = call(
        mixer_kernel,
        (
            shaped((COUNT, WIDTH), BF16),
            shaped((COUNT, WIDTH), BF16),
            shaped((1, COUNT), F32),
        ),
        [vmem()] * 10,
        [vmem()] * 3,
        [pltpu.VMEM((COUNT, WIDTH), F32)],
    )(
        inner,
        coup,
        steps,
        cums,
        first,
        drop,
        entry,
        gate_input,
        jnp.repeat(skip_gain, HDIM)[None, :],
        norm_gain[None, :],
    )

    owned, sums, iu2, id2, iu3, id3 = call(
        project_kernel,
        (shaped((TOK, D), F32), shaped((1, COUNT), F32), piece, piece, piece, piece),
        [vmem()] * 4 + [anyspace()] * 2,
        [vmem()] * 2 + [anyspace()] * 4,
        [
            pltpu.VMEM((2, 4, 128, D // 2), BF16),
            pltpu.VMEM((2, 6, 128, D // 4), BF16),
            pltpu.VMEM((2, 6, TOK, D // 4), BF16),
            pltpu.VMEM((2, 128, D // 2), BF16),
            pltpu.VMEM((2, 2, 128, D // 4), BF16),
            pltpu.VMEM((2, 2, TOK, D // 4), BF16),
            pltpu.VMEM((FLIGHT, 1, COUNT), F32),
            dma((24,)),
            dma((24,)),
            dma((FLIGHT,)),
            dma((FLIGHT,)),
            dma((4,)),
            dma((4,)),
        ],
        collective_id=1,
    )(byx, byy, out_weight, squares, iu1, id1)

    hidden, rows, weights = call(
        route_kernel,
        (
            shaped((TOK, D), F32),
            shaped((2, FLIGHT, CAP, D // 2), BF16),
            shaped((TOK, FLIGHT * CAP), BF16),
        ),
        [vmem()] * 7,
        [vmem()] * 3,
    )(owned, sums, residual, moe_gain[None, :], router_weight, routes, priority)

    back = call(
        expert_kernel,
        shaped((FLIGHT, 2, CAP, D // 2), BF16),
        [vmem()] + [anyspace()] * 8,
        anyspace(),
        [
            pltpu.VMEM((FLIGHT, 2, CAP, D // 2), BF16),
            pltpu.VMEM((RING, 2 * FLIGHT * CAP, SLICE), BF16),
            pltpu.VMEM((RING, SLICE, 2 * FFE), BF16),
            pltpu.VMEM((RING, SLICE, FFE), BF16),
            pltpu.VMEM((2 * FLIGHT * CAP, 2 * FFE), F32),
            pltpu.VMEM((2 * FLIGHT * CAP, 2 * FFE), BF16),
            pltpu.VMEM((2 * FLIGHT * CAP, 2 * FFE), BF16),
            pltpu.VMEM((FLIGHT, 2, CAP, D // 2), BF16),
            dma((2 * FLIGHT,)),
            dma((2 * FLIGHT,)),
            dma((2 * FLIGHT,)),
            dma((2 * FLIGHT,)),
            dma((10,)),
            dma((10,)),
            dma((7,)),
            dma((3,)),
            dma((1,)),
            dma((1,)),
        ],
        collective_id=2,
    )(rows, wi, iu1, id1, iu2, id2, iu3, id3, wo)

    moe_out = call(
        combine_kernel, shaped((TOK, D), F32), [vmem()] * 2, vmem()
    )(weights, back)
    return (hidden, moe_out)


def solution(mesh):
    placed = (
        P("ctx", "exp"),
        P("ctx", "exp"),
        P("ctx", None),
        P("ctx", "exp"),
        P(None, "exp"),
        P(),
        P("exp"),
        P("exp"),
        P("exp"),
        P("exp", None),
        P(("ctx", "exp"), None),
        P(),
        P(),
        P(("ctx", "exp"), None),
        P(("ctx", "exp"), None),
        P("exp", "ctx", None),
        P("exp", "ctx", None),
    )
    return jax.shard_map(
        body,
        mesh=mesh,
        in_specs=placed,
        out_specs=(P(("ctx", "exp"), None), P(("ctx", "exp"), None)),
        check_vma=False,
    )
```

```python
from types import SimpleNamespace

import jax
import jax.numpy as jnp
from jax import lax
from jax.experimental import pallas as pl
from jax.experimental.pallas import tpu as pltpu
from jax.sharding import PartitionSpec as P

HDIM = 64
STATE = 128
KCONV = 4
NEXP = 72
TOPK = 10
FFE = 768
SPAN = 256
INNER = 8192
D = 4096
HEADS = 8
WIDTH = 512
COUNT = 512
TOK = 32
CAP = 8
FLIGHT = 16
SLICE = 256
RING = 8
CHUNKS = 8
EDGE = 16
PLANE = 32
GROUPS = ((0, 1, 4, 2), (5, 3, 6, 7))

EPS = 1e-05
HIGH = lax.Precision.HIGHEST
F32 = jnp.float32
BF16 = jnp.bfloat16
MESH = pl.DeviceIdType.MESH
VMEM_LIMIT = 60 * 1024 * 1024


def vmem():
    return pl.BlockSpec(memory_space=pltpu.VMEM)


def anyspace():
    return pl.BlockSpec(memory_space=pl.ANY)


def shaped(shape, dtype):
    return jax.ShapeDtypeStruct(shape, dtype)


def silu(x):
    return x * jax.nn.sigmoid(x)


def where_am_i():
    c = lax.axis_index("ctx")
    e = lax.axis_index("exp")
    return lax.div(c, 2), lax.rem(c, 2), lax.div(e, 4), lax.rem(e, 4)


def up_down(z, core):
    up = lax.rem(z + 1, RING) * 2 + core
    down = lax.rem(z + RING - 1, RING) * 2 + core
    return up, down


def remote(src, dst, send, recv, device):
    return pltpu.make_async_remote_copy(
        src_ref=src,
        dst_ref=dst,
        send_sem=send,
        recv_sem=recv,
        device_id=device,
        device_id_type=MESH,
    )


def conv_part(src_ref, halo, weight_ref, pad_ref):
    count = src_ref.shape[0]
    pad_ref[0:EDGE, :] = halo
    pad_ref[EDGE : EDGE + count, :] = src_ref[...].astype(F32)
    first = EDGE - KCONV + 1
    total = weight_ref[0:1, :] * pad_ref[first : first + count, :]
    for k in range(1, KCONV):
        total = total + weight_ref[k : k + 1, :] * pad_ref[first + k : first + k + count, :]
    return silu(total).astype(BF16)


def expander():
    row = lax.broadcasted_iota(jnp.int32, (HEADS, WIDTH), 0)
    lane = lax.broadcasted_iota(jnp.int32, (HEADS, WIDTH), 1)
    return (lax.div(lane, HDIM) == row).astype(F32)


def spread_cols(values, expand):
    return lax.dot_general(
        values, expand, (((0,), (0,)), ((), ())), precision=HIGH, preferred_element_type=F32
    )


def spread_row(column, expand):
    return jnp.sum(column * expand, axis=0, keepdims=True)


def diagonal(row):
    n = row.shape[1]
    a = lax.broadcasted_iota(jnp.int32, (n, n), 0)
    b = lax.broadcasted_iota(jnp.int32, (n, n), 1)
    return jnp.sum(jnp.where(a == b, row, 0.0), axis=1, keepdims=True)


INPUTS = [
    "x",
    "cpl",
    "step",
    "conv",
    "conv_cpl",
    "decay",
    "skip",
    "norm_gain",
    "moe_gain",
    "routes",
    "priority",
    "gate_in",
    "out_w",
    "residual_in",
    "router_in",
    "wi",
    "wo",
]
OUTPUTS = ["hidden", "moe_out"]


def scratch():
    dma = pltpu.SemaphoreType.DMA
    V = pltpu.VMEM
    half, quarter = D // 2, D // 4
    return {
        "gate": V((COUNT, WIDTH), BF16),
        "w": V((WIDTH, D), BF16),
        "residual": V((TOK, D), BF16),
        "router": V((NEXP, D), BF16),
        "halo_x": V((EDGE, WIDTH), BF16),
        "halo_c": V((EDGE, 2 * STATE), BF16),
        "pad": V((COUNT + EDGE, WIDTH), F32),
        "pad_c": V((COUNT + EDGE, 2 * STATE), F32),
        "inner": V((COUNT, WIDTH), BF16),
        "coup": V((COUNT, 2 * STATE), BF16),
        "steps": V((HEADS, COUNT), F32),
        "cums": V((HEADS, COUNT), F32),
        "first": V((STATE, WIDTH), F32),
        "run": V((STATE, WIDTH), F32),
        "reach": V((1, WIDTH), F32),
        "drop": V((1, WIDTH), F32),
        "entry": V((STATE, WIDTH), F32),
        "gated": V((COUNT, WIDTH), F32),
        "growth": V((COUNT, WIDTH), F32),
        "byx": V((COUNT, WIDTH), BF16),
        "byy": V((COUNT, WIDTH), BF16),
        "squares": V((1, COUNT), F32),
        "sums": V((1, COUNT), F32),
        "mine": V((STATE, WIDTH), BF16),
        "theirs": V((STATE, WIDTH), BF16),
        "their_reach": V((1, WIDTH), F32),
        "arriving": V((STATE, WIDTH), BF16),
        "onward": V((STATE, WIDTH), BF16),
        "parts": V((2, 4, 128, half), BF16),
        "near": V((2, 6, 128, quarter), BF16),
        "far": V((2, 6, TOK, quarter), BF16),
        "joined": V((2, 128, half), BF16),
        "near_sum": V((2, 2, 128, quarter), BF16),
        "far_sum": V((2, 2, TOK, quarter), BF16),
        "all_squares": V((FLIGHT, 1, COUNT), F32),
        "owned": V((TOK, D), F32),
        "normed": V((2 * RING, TOK, SLICE), BF16),
        "share": V((TOK, FLIGHT * CAP), BF16),
        "rows": V((2, 2, FLIGHT, CAP, quarter), BF16),
        "landed": V((2, FLIGHT, 2, CAP, quarter), BF16),
        "tokens": V((RING, PLANE * CAP, SLICE), BF16),
        "ups": V((RING, SLICE, 2 * FFE), BF16),
        "downs": V((RING, SLICE, FFE), BF16),
        "units": V((PLANE * CAP, 2 * FFE), F32),
        "units_out": V((PLANE * CAP, 2 * FFE), BF16),
        "units_in": V((PLANE * CAP, 2 * FFE), BF16),
        "answers": V((2, FLIGHT, 2, CAP, quarter), BF16),
        "back": V((2, FLIGHT, 2, CAP, quarter), BF16),
        "load_sem": dma((6,)),
        "halo_send": dma((2,)),
        "halo_recv": dma((2,)),
        "pair_send": dma((3,)),
        "pair_recv": dma((3,)),
        "chain_send": dma((CHUNKS,)),
        "chain_recv": dma((CHUNKS,)),
        "relay_send": dma((CHUNKS,)),
        "hop_send": dma((17,)),
        "hop_recv": dma((17,)),
        "ring_send": dma((24,)),
        "ring_recv": dma((24,)),
        "sq_send": dma((FLIGHT,)),
        "sq_recv": dma((FLIGHT,)),
        "row_send": dma((2, PLANE)),
        "row_recv": dma((2, PLANE)),
        "back_send": dma((2, PLANE)),
        "back_recv": dma((2, PLANE)),
        "own_sem": dma((4,)),
    }


def layer_kernel(*refs):
    r = SimpleNamespace(**dict(zip(INPUTS + OUTPUTS + list(scratch()), refs, strict=True)))
    z, core, x, y = where_am_i()
    c = z * 2 + core
    me = x * 4 + y
    up, down = up_down(z, core)
    partner = z * 2 + 1 - core
    after = lax.rem(c + 1, 2 * RING)
    before = lax.rem(c + 2 * RING - 1, 2 * RING)
    cross = jnp.where(core == 0, before, after)

    def peer(i):
        return lax.rem(me + i, FLIGHT)

    def mate(i):
        other = lax.rem(me + lax.div(i, 2), FLIGHT)
        other_core = lax.rem(core + i, 2)
        return other, other_core, {"ctx": z * 2 + other_core, "exp": other}

    barrier = pltpu.get_barrier_semaphore()
    for other in (up, down, cross):
        pl.semaphore_signal(barrier, inc=1, device_id={"ctx": other}, device_id_type=MESH)

    def greet(i, carry):
        pl.semaphore_signal(barrier, inc=1, device_id=mate(i)[2], device_id_type=MESH)
        return carry

    lax.fori_loop(1, PLANE, greet, 0)
    loads = [
        pltpu.make_async_copy(src, dst, r.load_sem.at[i])
        for i, (src, dst) in enumerate(
            (
                (r.gate_in, r.gate),
                (r.out_w, r.w),
                (r.residual_in, r.residual),
                (r.router_in, r.router),
                (r.wi, r.ups.at[0]),
                (r.wo, r.downs.at[0]),
            )
        )
    ]
    for copy in loads:
        copy.start()

    raw = r.step[...]
    steps = jnp.maximum(raw, 0.0) + jnp.log1p(jnp.exp(-jnp.abs(raw)))
    r.steps[...] = steps
    rate = steps * (-jnp.exp(diagonal(r.decay[...])))
    pl.semaphore_wait(barrier, PLANE + 2)

    halos = [
        remote(
            r.x.at[pl.ds(COUNT - EDGE, EDGE)],
            r.halo_x,
            r.halo_send.at[0],
            r.halo_recv.at[0],
            {"ctx": after},
        ),
        remote(
            r.cpl.at[pl.ds(COUNT - EDGE, EDGE)],
            r.halo_c,
            r.halo_send.at[1],
            r.halo_recv.at[1],
            {"ctx": after},
        ),
    ]

    def hop(slot, src, dst, toward):
        return remote(src, dst, r.hop_send.at[slot], r.hop_recv.at[slot], {"ctx": toward})

    cut = SLICE // 2
    low_rows, high_rows = pl.ds(0, cut), pl.ds(cut, cut)
    up_early = hop(0, r.wi.at[low_rows], r.ups.at[1, low_rows], up)
    up_late = hop(1, r.wi.at[high_rows], r.ups.at[1, high_rows], up)
    ups_up = [None]
    ups_down = [hop(2, r.wi, r.ups.at[4], down)]
    downs_up = [hop(3, r.wo, r.downs.at[1], up)]
    downs_down = [hop(4, r.wo, r.downs.at[4], down)]
    for n in (1, 2):
        base = 4 * n + 1
        ups_up.append(hop(base, r.ups.at[n], r.ups.at[n + 1], up))
        ups_down.append(hop(base + 1, r.ups.at[n + 3], r.ups.at[n + 4], down))
        downs_up.append(hop(base + 2, r.downs.at[n], r.downs.at[n + 1], up))
        downs_down.append(hop(base + 3, r.downs.at[n + 3], r.downs.at[n + 4], down))
    ups_up.append(hop(13, r.ups.at[3, low_rows], r.ups.at[7, low_rows], up))
    ups_down.append(hop(14, r.ups.at[6, high_rows], r.ups.at[7, high_rows], down))
    downs_up.append(hop(15, r.downs.at[3, low_rows], r.downs.at[7, low_rows], up))
    downs_down.append(hop(16, r.downs.at[6, high_rows], r.downs.at[7, high_rows], down))

    @pl.when(c < 2 * RING - 1)
    def _():
        for copy in halos:
            copy.start()

    hold = (core == 1) & (z < RING - 1)
    up_early.start()
    ups_down[0].start()
    downs_down[0].start()

    @pl.when(jnp.logical_not(hold) | (z >= 4))
    def _():
        up_late.start()

    @pl.when(jnp.logical_not(hold))
    def _():
        downs_up[0].start()

    row = lax.broadcasted_iota(jnp.int32, (SPAN, SPAN), 0)
    col = lax.broadcasted_iota(jnp.int32, (SPAN, SPAN), 1)
    upper = (row <= col).astype(F32)
    above = row >= col
    expand = expander()
    for b in range(COUNT // SPAN):
        part = slice(b * SPAN, (b + 1) * SPAN)
        r.cums[:, part] = jnp.dot(
            rate[:, part], upper, precision=HIGH, preferred_element_type=F32
        )

    @pl.when(c > 0)
    def _():
        for copy in halos:
            copy.wait_recv()

    @pl.when(c == 0)
    def _():
        r.halo_x[...] = jnp.zeros_like(r.halo_x)
        r.halo_c[...] = jnp.zeros_like(r.halo_c)

    r.inner[...] = conv_part(r.x, r.halo_x[...].astype(F32), r.conv, r.pad)
    r.coup[...] = conv_part(r.cpl, r.halo_c[...].astype(F32), r.conv_cpl, r.pad_c)
    states = []
    drops = []
    for b in range(COUNT // SPAN):
        part = slice(b * SPAN, (b + 1) * SPAN)
        cums = r.cums[:, part]
        last = cums[:, SPAN - 1 : SPAN]
        tail = jnp.exp(last - cums) * r.steps[:, part]
        weighted = (r.inner[part, :].astype(F32) * spread_cols(tail, expand)).astype(BF16)
        states.append(
            lax.dot_general(
                r.coup[part, :STATE],
                weighted,
                (((0,), (0,)), ((), ())),
                preferred_element_type=F32,
            )
        )
        drops.append(spread_row(jnp.exp(last), expand))
    r.first[...] = states[0]
    run = drops[1] * states[0] + states[1]
    r.run[...] = run
    r.reach[...] = drops[0] * drops[1]
    r.drop[...] = drops[0]
    r.mine[...] = run.astype(BF16)

    def local_part():
        lane = lax.broadcasted_iota(jnp.int32, (SPAN, 2 * HDIM), 1)
        skip = spread_row(diagonal(r.skip[...]), expand)
        for b in range(COUNT // SPAN):
            part = slice(b * SPAN, (b + 1) * SPAN)
            scores = lax.dot_general(
                r.coup[part, STATE:],
                r.coup[part, :STATE],
                (((1,), (1,)), ((), ())),
                preferred_element_type=F32,
            )
            scores = jnp.where(above, scores, 0.0)
            cums = r.cums[:, part]
            turned = cums.T
            opened = silu(r.gate[part, :].astype(F32))
            r.growth[part, :] = spread_cols(jnp.exp(cums), expand) * opened
            for pair in range(HEADS // 2):
                cols = slice(pair * 2 * HDIM, (pair + 1) * 2 * HDIM)
                values = r.inner[part, cols]
                halves = []
                for h in (2 * pair, 2 * pair + 1):
                    spread = turned[:, h : h + 1] - cums[h : h + 1, :]
                    decay = jnp.exp(jnp.where(above, spread, 0.0))
                    mixing = (scores * decay * r.steps[h : h + 1, part]).astype(BF16)
                    halves.append(jnp.dot(mixing, values, preferred_element_type=F32))
                local = jnp.where(lane < HDIM, halves[0], halves[1])
                mixed = local + skip[:, cols] * values.astype(F32)
                r.gated[part, cols] = mixed * opened[:, cols]

    pairs = [
        remote(r.mine, r.theirs, r.pair_send.at[0], r.pair_recv.at[0], {"ctx": partner}),
        remote(r.reach, r.their_reach, r.pair_send.at[1], r.pair_recv.at[1], {"ctx": partner}),
    ]
    lines = STATE // CHUNKS
    spans = [pl.ds(i * lines, lines) for i in range(CHUNKS)]
    ahead = [
        remote(r.onward.at[s], r.arriving.at[s], r.chain_send.at[i], r.chain_recv.at[i], {"ctx": up})
        for i, s in enumerate(spans)
    ]
    relays = [
        remote(
            r.arriving.at[s],
            r.arriving.at[s],
            r.relay_send.at[i],
            r.chain_recv.at[i],
            {"ctx": partner},
        )
        for i, s in enumerate(spans)
    ]

    @pl.when(core == 0)
    def _():
        for copy in pairs:
            copy.start()

    loads[0].wait()
    early = z >= 3

    @pl.when(early)
    def _():
        local_part()

    @pl.when((core == 0) & (z == 0))
    def _():
        r.entry[...] = jnp.zeros_like(r.entry)

    @pl.when((core == 0) & (z > 0))
    def _():
        for i, s in enumerate(spans):
            relays[i].wait_recv()
            r.entry[s, :] = r.arriving[s, :].astype(F32)

    @pl.when(core == 1)
    def _():
        for copy in pairs:
            copy.wait_recv()

        @pl.when(z == 0)
        def _():
            for i, s in enumerate(spans):
                start = r.theirs[s, :].astype(F32)
                r.onward[s, :] = (r.reach[...] * start + r.run[s, :]).astype(BF16)
                ahead[i].start()
                r.entry[s, :] = start

        @pl.when(z > 0)
        def _():
            for i, s in enumerate(spans):
                start = r.theirs[s, :].astype(F32)
                ahead[i].wait_recv()
                inside = r.their_reach[...] * r.arriving[s, :].astype(F32) + start
                r.onward[s, :] = (r.reach[...] * inside + r.run[s, :]).astype(BF16)

                @pl.when(z < RING - 1)
                def _():
                    ahead[i].start()

                relays[i].start()
                r.entry[s, :] = inside

    @pl.when(hold & (z < 4))
    def _():
        up_late.start()

    @pl.when(hold)
    def _():
        downs_up[0].start()

    @pl.when(jnp.logical_not(early))
    def _():
        local_part()

    for b in range(COUNT // SPAN):
        part = slice(b * SPAN, (b + 1) * SPAN)
        entry = r.entry[...]
        if b == 1:
            entry = r.drop[...] * entry + r.first[...]
        carried = jnp.dot(r.coup[part, STATE:], entry.astype(BF16), preferred_element_type=F32)
        gated = r.gated[part, :] + carried * r.growth[part, :]
        r.gated[part, :] = gated
        scaled = (gated * r.norm_gain[...]).astype(BF16)
        r.byx[part, :] = scaled
        for k in range(SPAN // TOK):
            at_x, at_y = divmod(b * (SPAN // TOK) + k, 4)
            r.byy[(at_y * 4 + at_x) * TOK : (at_y * 4 + at_x + 1) * TOK, :] = scaled[
                k * TOK : (k + 1) * TOK, :
            ]

    half = D // 2
    quarter = half // 2
    low = pl.ds(0, quarter)
    high = pl.ds(quarter, quarter)

    def squares_copy(i):
        return remote(
            r.squares, r.all_squares.at[i], r.sq_send.at[i], r.sq_recv.at[i], {"exp": peer(i)}
        )

    def along_x(by):
        return {"exp": lax.rem(x + by, 4) * 4 + y}

    def along_y(by):
        return {"exp": x * 4 + lax.rem(y + by, 4)}

    def message(stage, side, number, src):
        slot = stage * 12 + side * 6 + number
        toward = along_x if side == stage else along_y
        landing = (r.near if stage == 0 else r.far).at[side, number]
        return remote(
            src,
            landing,
            r.ring_send.at[slot],
            r.ring_recv.at[slot],
            toward(1 if number % 2 == 0 else 3),
        )

    def block(stage, side, offset):
        if stage == 0:
            return r.parts.at[side, offset]
        place = y if side == 0 else x
        start = pl.multiple_of(lax.rem(place + offset, 4) * TOK, TOK)
        return r.joined.at[side, pl.ds(start, TOK)]

    def sources(stage, side):
        across = block(stage, side, 2)
        right = block(stage, side, 1)
        left = block(stage, side, 3)
        sums = r.near_sum if stage == 0 else r.far_sum
        return [
            across.at[:, low],
            across.at[:, high],
            right.at[:, high],
            left.at[:, low],
            sums.at[side, 0],
            sums.at[side, 1],
        ]

    copies = [
        [
            [message(stage, side, n, src) for n, src in enumerate(sources(stage, side))]
            for side in range(2)
        ]
        for stage in range(2)
    ]

    def multiply(side, offset):
        rows_ref = r.byx if side == 0 else r.byy
        place = x if side == 0 else y
        start = pl.multiple_of(lax.rem(place + offset, 4) * 128, 128)
        rows = rows_ref[pl.ds(start, 128), :]

        def one(i, carry):
            source = pl.ds(pl.multiple_of(side * half + i * 512, 512), 512)
            target = pl.ds(pl.multiple_of(i * 512, 512), 512)
            r.parts[side, offset, :, target] = jnp.dot(
                rows, r.w[:, source], preferred_element_type=F32
            ).astype(BF16)
            return carry

        lax.fori_loop(0, half // 512, one, 0)

    def pass_on(stage, side):
        landing = r.near if stage == 0 else r.far
        sums = r.near_sum if stage == 0 else r.far_sum
        copies[stage][side][0].wait_recv()
        sums[side, 0] = (
            block(stage, side, 1)[:, low].astype(F32) + landing[side, 0].astype(F32)
        ).astype(BF16)
        copies[stage][side][4].start()
        copies[stage][side][1].wait_recv()
        sums[side, 1] = (
            block(stage, side, 3)[:, high].astype(F32) + landing[side, 1].astype(F32)
        ).astype(BF16)
        copies[stage][side][5].start()

    def collect(stage, side):
        landing = r.near if stage == 0 else r.far
        for n in (2, 3, 4, 5):
            copies[stage][side][n].wait_recv()
        own = block(stage, side, 0)
        first = own[:, low].astype(F32) + landing[side, 4].astype(F32)
        first = first + landing[side, 3].astype(F32)
        second = own[:, high].astype(F32) + landing[side, 2].astype(F32)
        second = second + landing[side, 5].astype(F32)
        return first, second

    loads[1].wait()
    for side in range(2):
        multiply(side, 2)
        copies[0][side][0].start()
        copies[0][side][1].start()
    for side in range(2):
        multiply(side, 1)
        copies[0][side][2].start()
        multiply(side, 3)
        copies[0][side][3].start()
    up_early.wait_recv()
    up_late.wait_recv()
    ups_up[1].start()
    ups_down[0].wait_recv()
    ups_down[1].start()
    for side in range(2):
        pass_on(0, side)
    for side in range(2):
        multiply(side, 0)
    gated = r.gated[...]
    r.squares[...] = lax.dot_general(
        jnp.ones((8, WIDTH), F32),
        gated * gated,
        (((1,), (1,)), ((), ())),
        precision=HIGH,
        preferred_element_type=F32,
    )[0:1, :]

    def send_squares(i, carry):
        squares_copy(i).start()
        return carry

    lax.fori_loop(1, FLIGHT, send_squares, 0)
    downs_up[0].wait_recv()
    downs_up[1].start()
    downs_down[0].wait_recv()
    downs_down[1].start()
    for side in range(2):
        first, second = collect(0, side)
        r.joined[side, :, low] = first.astype(BF16)
        r.joined[side, :, high] = second.astype(BF16)
        for n in range(4):
            copies[1][side][n].start()
    for side in range(2):
        pass_on(1, side)
    for side in range(2):
        first, second = collect(1, side)
        r.owned[:, pl.ds(side * half, quarter)] = first
        r.owned[:, pl.ds(side * half + quarter, quarter)] = second
    r.all_squares[0] = r.squares[...]

    def take_squares(i, carry):
        squares_copy(i).wait()
        return carry

    lax.fori_loop(1, FLIGHT, take_squares, 0)
    total = r.all_squares[0]
    for i in range(1, FLIGHT):
        total = total + r.all_squares[i]

    loads[2].wait()
    loads[3].wait()
    wide_row = lax.broadcasted_iota(jnp.int32, (TOK, COUNT), 0)
    wide_col = lax.broadcasted_iota(jnp.int32, (TOK, COUNT), 1)
    squares = jnp.sum(
        jnp.where(wide_col == me * TOK + wide_row, total, 0.0), axis=1, keepdims=True
    )
    hidden = r.residual[...].astype(F32) + r.owned[...] * lax.rsqrt(squares / INNER + EPS)
    r.hidden[...] = hidden
    mean = jnp.sum(hidden * hidden, axis=1, keepdims=True) / D
    normed = (hidden * lax.rsqrt(mean + EPS) * r.moe_gain[...]).astype(BF16)
    for s in range(2 * RING):
        r.normed[s] = normed[:, s * SLICE : (s + 1) * SLICE]
    expert = lax.broadcasted_iota(jnp.int32, (TOK, NEXP), 1)
    named = expert < 0
    for k in range(TOPK):
        choice = diagonal(r.routes[k : k + 1, :].astype(F32))
        named = named | (choice.astype(jnp.int32) == expert)
    order = r.priority[...].astype(F32)
    earlier = (order < diagonal(order)).astype(F32).astype(BF16)
    rank = jnp.dot(earlier, named.astype(F32).astype(BF16), preferred_element_type=F32)
    key = jnp.where(named, rank, 99.0).astype(BF16)
    lanes = FLIGHT * CAP
    widen_row = lax.broadcasted_iota(jnp.int32, (NEXP, lanes), 0)
    widen_col = lax.broadcasted_iota(jnp.int32, (NEXP, lanes), 1)
    widen = (lax.div(widen_col, CAP) == widen_row).astype(F32).astype(BF16)
    key_wide = jnp.dot(key, widen, preferred_element_type=F32)
    slot = lax.rem(lax.broadcasted_iota(jnp.int32, (TOK, lanes), 1), CAP).astype(F32)
    chosen = (key_wide == slot).astype(F32)
    pick = chosen.astype(BF16)

    def source(n):
        if n <= 3:
            return lax.rem(z + RING - n, RING)
        if n <= 6:
            return lax.rem(z + n - 3, RING)
        return lax.rem(z + 4, RING)

    def row_copy(g, i):
        other, other_core, device = mate(i)
        return remote(
            r.rows.at[g, other_core, other],
            r.landed.at[g, me, core],
            r.row_send.at[g, i],
            r.row_recv.at[g, i],
            device,
        )

    own_rows = []
    for g in range(2):
        for j in range(2):
            for k, n in enumerate(GROUPS[g]):
                taken = lax.dot_general(
                    pick,
                    r.normed[2 * source(n) + j],
                    (((0,), (0,)), ((), ())),
                    preferred_element_type=F32,
                )
                r.rows[g, j, :, :, k * SLICE : (k + 1) * SLICE] = taken.reshape(
                    FLIGHT, CAP, SLICE
                ).astype(BF16)

        def start_rows(i, carry):
            row_copy(g, i).start()
            return carry

        lax.fori_loop(1, PLANE, start_rows, 0)
        own_rows.append(
            pltpu.make_async_copy(
                r.rows.at[g, core, me], r.landed.at[g, me, core], r.own_sem.at[g]
            )
        )
        own_rows[g].start()

    ups_up[1].wait_recv()
    ups_up[2].start()
    ups_down[1].wait_recv()
    ups_down[2].start()
    logits = lax.dot_general(
        normed, r.router[...], (((1,), (1,)), ((), ())), preferred_element_type=F32
    )
    raised = jnp.where(named, jnp.exp(logits), 0.0)
    share = (raised / jnp.sum(raised, axis=1, keepdims=True)).astype(BF16)
    share_wide = jnp.dot(share, widen, preferred_element_type=F32)
    r.share[...] = (chosen * share_wide).astype(BF16)
    downs_up[1].wait_recv()
    downs_up[2].start()
    downs_down[1].wait_recv()
    downs_down[2].start()

    loads[4].wait()
    loads[5].wait()
    for g in range(2):
        if g == 1:
            ups_up[2].wait_recv()
            ups_up[3].start()
            ups_down[2].wait_recv()
            ups_down[3].start()
        own_rows[g].wait()

        def take_rows(i, carry):
            row_copy(g, i).wait()
            return carry

        lax.fori_loop(1, PLANE, take_rows, 0)
        for k, n in enumerate(GROUPS[g]):
            cols = slice(k * SLICE, (k + 1) * SLICE)
            r.tokens[n] = (
                r.landed[g, :, :, :, cols].astype(F32).reshape(PLANE * CAP, SLICE).astype(BF16)
            )

        def gate_up(i, carry):
            cols = pl.ds(pl.multiple_of(i * 256, 256), 256)
            total = None if g == 0 else r.units[:, cols]
            for n in GROUPS[g]:
                if n == 7:
                    continue
                value = jnp.dot(r.tokens[n], r.ups[n, :, cols], preferred_element_type=F32)
                total = value if total is None else total + value
            r.units[:, cols] = total
            return carry

        lax.fori_loop(0, 2 * FFE // 256, gate_up, 0)
    downs_up[2].wait_recv()
    downs_up[3].start()
    downs_down[2].wait_recv()
    downs_down[3].start()
    ups_up[3].wait_recv()
    ups_down[3].wait_recv()

    def last_slice(i, carry):
        cols = pl.ds(pl.multiple_of(i * 256, 256), 256)
        total = r.units[:, cols] + jnp.dot(
            r.tokens[7], r.ups[7, :, cols], preferred_element_type=F32
        )
        r.units[:, cols] = total
        r.units_out[:, cols] = total.astype(BF16)
        return carry

    lax.fori_loop(0, 2 * FFE // 256, last_slice, 0)
    swap = remote(r.units_out, r.units_in, r.pair_send.at[2], r.pair_recv.at[2], {"ctx": partner})
    swap.start()
    swap.wait()
    gate = r.units[:, :FFE] + r.units_in[:, :FFE].astype(F32)
    lift = r.units[:, FFE:] + r.units_in[:, FFE:].astype(F32)
    activated = (silu(gate) * lift).astype(BF16)

    def back_copy(g, i):
        other, other_core, device = mate(i)
        return remote(
            r.answers.at[g, other, other_core],
            r.back.at[g, me, core],
            r.back_send.at[g, i],
            r.back_recv.at[g, i],
            device,
        )

    own_back = []
    for g in range(2):
        for k, n in enumerate(GROUPS[g]):
            if n == 7:
                downs_up[3].wait_recv()
                downs_down[3].wait_recv()
            values = lax.dot_general(
                activated, r.downs[n], (((1,), (1,)), ((), ())), preferred_element_type=F32
            )
            r.answers[g, :, :, :, k * SLICE : (k + 1) * SLICE] = values.reshape(
                FLIGHT, 2, CAP, SLICE
            ).astype(BF16)

        def start_back(i, carry):
            back_copy(g, i).start()
            return carry

        lax.fori_loop(1, PLANE, start_back, 0)
        own_back.append(
            pltpu.make_async_copy(
                r.answers.at[g, me, core], r.back.at[g, me, core], r.own_sem.at[2 + g]
            )
        )
        own_back[g].start()

    for g in range(2):
        own_back[g].wait()

        def take_back(i, carry):
            back_copy(g, i).wait()
            return carry

        lax.fori_loop(1, PLANE, take_back, 0)
        weights = r.share[...]
        for j in range(2):
            rows = r.back[g, :, j].astype(F32).reshape(FLIGHT * CAP, quarter).astype(BF16)
            total = jnp.dot(weights, rows, preferred_element_type=F32)
            for k, n in enumerate(GROUPS[g]):
                place = pl.multiple_of((2 * source(n) + j) * SLICE, SLICE)
                r.moe_out[:, pl.ds(place, SLICE)] = total[:, k * SLICE : (k + 1) * SLICE]

    @pl.when(c < 2 * RING - 1)
    def _():
        for copy in halos:
            copy.wait_send()

    @pl.when(core == 0)
    def _():
        for copy in pairs:
            copy.wait_send()

    @pl.when(hold)
    def _():
        for copy in ahead:
            copy.wait_send()

    @pl.when((core == 1) & (z > 0))
    def _():
        for copy in relays:
            copy.wait_send()

    for stage in range(2):
        for side in range(2):
            for copy in copies[stage][side]:
                copy.wait_send()
    for copy in [up_early, up_late] + ups_up[1:] + ups_down + downs_up + downs_down:
        copy.wait_send()


def body(
    inner_input,
    gate_input,
    coupling_input,
    step_input,
    conv_inner,
    conv_coupling,
    decay_log,
    skip_gain,
    norm_gain,
    out_weight,
    residual,
    moe_gain,
    router_weight,
    routes,
    priority,
    expert_in,
    expert_out,
):
    return pl.pallas_call(
        layer_kernel,
        out_shape=(shaped((TOK, D), F32), shaped((TOK, D), F32)),
        in_specs=[vmem()] * 11 + [anyspace()] * 6,
        out_specs=(vmem(), vmem()),
        scratch_shapes=list(scratch().values()),
        compiler_params=pltpu.CompilerParams(
            vmem_limit_bytes=VMEM_LIMIT, collective_id=0, has_side_effects=True
        ),
    )(
        inner_input,
        coupling_input,
        step_input.T,
        conv_inner,
        conv_coupling,
        decay_log[None, :],
        skip_gain[None, :],
        norm_gain[None, :],
        moe_gain[None, :],
        routes.T,
        priority,
        gate_input,
        out_weight,
        residual,
        router_weight.T,
        expert_in[0],
        expert_out[0],
    )


def solution(mesh):
    placed = (
        P("ctx", "exp"),
        P("ctx", "exp"),
        P("ctx", None),
        P("ctx", "exp"),
        P(None, "exp"),
        P(),
        P("exp"),
        P("exp"),
        P("exp"),
        P("exp", None),
        P(("ctx", "exp"), None),
        P(),
        P(),
        P(("ctx", "exp"), None),
        P(("ctx", "exp"), None),
        P("exp", "ctx", None),
        P("exp", "ctx", None),
    )
    return jax.shard_map(
        body,
        mesh=mesh,
        in_specs=placed,
        out_specs=(P(("ctx", "exp"), None), P(("ctx", "exp"), None)),
        check_vma=False,
    )
```

```python
from types import SimpleNamespace

import jax
import jax.numpy as jnp
from jax import lax
from jax.experimental import pallas as pl
from jax.experimental.pallas import tpu as pltpu
from jax.sharding import PartitionSpec as P

HDIM = 64
STATE = 128
KCONV = 4
NEXP = 72
TOPK = 10
FFE = 768
SPAN = 256
INNER = 8192
D = 4096
HEADS = 8
WIDTH = 512
COUNT = 512
TOK = 32
CAP = 8
FLIGHT = 16
SLICE = 256
RING = 8
CHUNKS = 8
EDGE = 16
PLANE = 32
GROUPS = ((0, 1, 4, 2), (5, 3, 6, 7))

EPS = 1e-05
HIGH = lax.Precision.HIGHEST
F32 = jnp.float32
BF16 = jnp.bfloat16
MESH = pl.DeviceIdType.MESH
VMEM_LIMIT = 60 * 1024 * 1024


def vmem():
    return pl.BlockSpec(memory_space=pltpu.VMEM)


def anyspace():
    return pl.BlockSpec(memory_space=pl.ANY)


def shaped(shape, dtype):
    return jax.ShapeDtypeStruct(shape, dtype)


def silu(x):
    return x * jax.nn.sigmoid(x)


def where_am_i():
    c = lax.axis_index("ctx")
    e = lax.axis_index("exp")
    return lax.div(c, 2), lax.rem(c, 2), lax.div(e, 4), lax.rem(e, 4)


def up_down(z, core):
    up = lax.rem(z + 1, RING) * 2 + core
    down = lax.rem(z + RING - 1, RING) * 2 + core
    return up, down


def remote(src, dst, send, recv, device):
    return pltpu.make_async_remote_copy(
        src_ref=src,
        dst_ref=dst,
        send_sem=send,
        recv_sem=recv,
        device_id=device,
        device_id_type=MESH,
    )


def conv_part(src_ref, halo, weight_ref, pad_ref):
    count = src_ref.shape[0]
    pad_ref[0:EDGE, :] = halo
    pad_ref[EDGE : EDGE + count, :] = src_ref[...].astype(F32)
    first = EDGE - KCONV + 1
    total = weight_ref[0:1, :] * pad_ref[first : first + count, :]
    for k in range(1, KCONV):
        total = total + weight_ref[k : k + 1, :] * pad_ref[first + k : first + k + count, :]
    return silu(total).astype(BF16)


def expander():
    row = lax.broadcasted_iota(jnp.int32, (HEADS, WIDTH), 0)
    lane = lax.broadcasted_iota(jnp.int32, (HEADS, WIDTH), 1)
    return (lax.div(lane, HDIM) == row).astype(F32)


def spread_cols(values, expand):
    return lax.dot_general(
        values, expand, (((0,), (0,)), ((), ())), precision=HIGH, preferred_element_type=F32
    )


def spread_row(column, expand):
    return jnp.sum(column * expand, axis=0, keepdims=True)


def diagonal(row):
    n = row.shape[1]
    a = lax.broadcasted_iota(jnp.int32, (n, n), 0)
    b = lax.broadcasted_iota(jnp.int32, (n, n), 1)
    return jnp.sum(jnp.where(a == b, row, 0.0), axis=1, keepdims=True)


INPUTS = [
    "x",
    "cpl",
    "step",
    "conv",
    "conv_cpl",
    "decay",
    "skip",
    "norm_gain",
    "moe_gain",
    "routes",
    "priority",
    "gate_in",
    "out_w",
    "residual_in",
    "router_in",
    "wi",
    "wo",
]
OUTPUTS = ["hidden", "moe_out"]


def scratch():
    dma = pltpu.SemaphoreType.DMA
    V = pltpu.VMEM
    half, quarter = D // 2, D // 4
    return {
        "gate": V((COUNT, WIDTH), BF16),
        "w": V((WIDTH, D), BF16),
        "residual": V((TOK, D), BF16),
        "router": V((NEXP, D), BF16),
        "halo_x": V((EDGE, WIDTH), BF16),
        "halo_c": V((EDGE, 2 * STATE), BF16),
        "pad": V((COUNT + EDGE, WIDTH), F32),
        "pad_c": V((COUNT + EDGE, 2 * STATE), F32),
        "inner": V((COUNT, WIDTH), BF16),
        "coup": V((COUNT, 2 * STATE), BF16),
        "steps": V((HEADS, COUNT), F32),
        "cums": V((HEADS, COUNT), F32),
        "first": V((STATE, WIDTH), F32),
        "run": V((STATE, WIDTH), F32),
        "reach": V((1, WIDTH), F32),
        "drop": V((1, WIDTH), F32),
        "entry": V((STATE, WIDTH), F32),
        "gated": V((COUNT, WIDTH), F32),
        "growth": V((COUNT, WIDTH), F32),
        "byx": V((COUNT, WIDTH), BF16),
        "byy": V((COUNT, WIDTH), BF16),
        "squares": V((1, COUNT), F32),
        "sums": V((1, COUNT), F32),
        "mine": V((STATE, WIDTH), BF16),
        "theirs": V((STATE, WIDTH), BF16),
        "their_reach": V((1, WIDTH), F32),
        "arriving": V((STATE, WIDTH), BF16),
        "onward": V((STATE, WIDTH), BF16),
        "parts": V((2, 4, 128, half), BF16),
        "near": V((2, 6, 128, quarter), BF16),
        "far": V((2, 6, TOK, quarter), BF16),
        "joined": V((2, 128, half), BF16),
        "near_sum": V((2, 2, 128, quarter), BF16),
        "far_sum": V((2, 2, TOK, quarter), BF16),
        "all_squares": V((FLIGHT, 1, COUNT), F32),
        "owned": V((TOK, D), F32),
        "normed": V((2 * RING, TOK, SLICE), BF16),
        "share": V((TOK, FLIGHT * CAP), BF16),
        "rows": V((2, 2, FLIGHT, CAP, quarter), BF16),
        "landed": V((2, FLIGHT, 2, CAP, quarter), BF16),
        "tokens": V((RING, PLANE * CAP, SLICE), BF16),
        "ups": V((RING, SLICE, 2 * FFE), BF16),
        "downs": V((RING, SLICE, FFE), BF16),
        "units": V((PLANE * CAP, 2 * FFE), F32),
        "units_out": V((PLANE * CAP, 2 * FFE), BF16),
        "units_in": V((PLANE * CAP, 2 * FFE), BF16),
        "answers": V((2, FLIGHT, 2, CAP, quarter), BF16),
        "back": V((2, FLIGHT, 2, CAP, quarter), BF16),
        "load_sem": dma((6,)),
        "halo_send": dma((2,)),
        "halo_recv": dma((2,)),
        "pair_send": dma((3,)),
        "pair_recv": dma((3,)),
        "chain_send": dma((CHUNKS,)),
        "chain_recv": dma((CHUNKS,)),
        "relay_send": dma((CHUNKS,)),
        "hop_send": dma((17,)),
        "hop_recv": dma((17,)),
        "ring_send": dma((24,)),
        "ring_recv": dma((24,)),
        "sq_send": dma((FLIGHT,)),
        "sq_recv": dma((FLIGHT,)),
        "row_send": dma((2, PLANE)),
        "row_recv": dma((2, PLANE)),
        "back_send": dma((2, PLANE)),
        "back_recv": dma((2, PLANE)),
        "own_sem": dma((4,)),
    }


def layer_kernel(*refs):
    r = SimpleNamespace(**dict(zip(INPUTS + OUTPUTS + list(scratch()), refs, strict=True)))
    z, core, x, y = where_am_i()
    c = z * 2 + core
    me = x * 4 + y
    up, down = up_down(z, core)
    partner = z * 2 + 1 - core
    after = lax.rem(c + 1, 2 * RING)
    before = lax.rem(c + 2 * RING - 1, 2 * RING)
    cross = jnp.where(core == 0, before, after)

    def peer(i):
        return lax.rem(me + i, FLIGHT)

    def mate(i):
        other = lax.rem(me + lax.div(i, 2), FLIGHT)
        other_core = lax.rem(core + i, 2)
        return other, other_core, {"ctx": z * 2 + other_core, "exp": other}

    barrier = pltpu.get_barrier_semaphore()
    for other in (up, down, cross):
        pl.semaphore_signal(barrier, inc=1, device_id={"ctx": other}, device_id_type=MESH)

    def greet(i, carry):
        pl.semaphore_signal(barrier, inc=1, device_id=mate(i)[2], device_id_type=MESH)
        return carry

    lax.fori_loop(1, PLANE, greet, 0)
    loads = [
        pltpu.make_async_copy(src, dst, r.load_sem.at[i])
        for i, (src, dst) in enumerate(
            (
                (r.gate_in, r.gate),
                (r.out_w, r.w),
                (r.residual_in, r.residual),
                (r.router_in, r.router),
                (r.wi, r.ups.at[0]),
                (r.wo, r.downs.at[0]),
            )
        )
    ]
    for copy in loads:
        copy.start()

    raw = r.step[...]
    steps = jnp.maximum(raw, 0.0) + jnp.log1p(jnp.exp(-jnp.abs(raw)))
    r.steps[...] = steps
    rate = steps * (-jnp.exp(diagonal(r.decay[...])))
    pl.semaphore_wait(barrier, PLANE + 2)

    halos = [
        remote(
            r.x.at[pl.ds(COUNT - EDGE, EDGE)],
            r.halo_x,
            r.halo_send.at[0],
            r.halo_recv.at[0],
            {"ctx": after},
        ),
        remote(
            r.cpl.at[pl.ds(COUNT - EDGE, EDGE)],
            r.halo_c,
            r.halo_send.at[1],
            r.halo_recv.at[1],
            {"ctx": after},
        ),
    ]

    def hop(slot, src, dst, toward):
        return remote(src, dst, r.hop_send.at[slot], r.hop_recv.at[slot], {"ctx": toward})

    cut = SLICE // 2
    low_rows, high_rows = pl.ds(0, cut), pl.ds(cut, cut)
    up_early = hop(0, r.wi.at[low_rows], r.ups.at[1, low_rows], up)
    up_late = hop(1, r.wi.at[high_rows], r.ups.at[1, high_rows], up)
    ups_up = [None]
    ups_down = [hop(2, r.wi, r.ups.at[4], down)]
    downs_up = [hop(3, r.wo, r.downs.at[1], up)]
    downs_down = [hop(4, r.wo, r.downs.at[4], down)]
    for n in (1, 2):
        base = 4 * n + 1
        ups_up.append(hop(base, r.ups.at[n], r.ups.at[n + 1], up))
        ups_down.append(hop(base + 1, r.ups.at[n + 3], r.ups.at[n + 4], down))
        downs_up.append(hop(base + 2, r.downs.at[n], r.downs.at[n + 1], up))
        downs_down.append(hop(base + 3, r.downs.at[n + 3], r.downs.at[n + 4], down))
    ups_up.append(hop(13, r.ups.at[3, low_rows], r.ups.at[7, low_rows], up))
    ups_down.append(hop(14, r.ups.at[6, high_rows], r.ups.at[7, high_rows], down))
    downs_up.append(hop(15, r.downs.at[3, low_rows], r.downs.at[7, low_rows], up))
    downs_down.append(hop(16, r.downs.at[6, high_rows], r.downs.at[7, high_rows], down))

    @pl.when(c < 2 * RING - 1)
    def _():
        for copy in halos:
            copy.start()

    hold = (core == 1) & (z < RING - 1)
    up_early.start()
    ups_down[0].start()
    downs_down[0].start()

    @pl.when(jnp.logical_not(hold) | (z >= 4))
    def _():
        up_late.start()

    @pl.when(jnp.logical_not(hold))
    def _():
        downs_up[0].start()

    row = lax.broadcasted_iota(jnp.int32, (SPAN, SPAN), 0)
    col = lax.broadcasted_iota(jnp.int32, (SPAN, SPAN), 1)
    upper = (row <= col).astype(F32)
    above = row >= col
    expand = expander()
    for b in range(COUNT // SPAN):
        part = slice(b * SPAN, (b + 1) * SPAN)
        r.cums[:, part] = jnp.dot(
            rate[:, part], upper, precision=HIGH, preferred_element_type=F32
        )

    @pl.when(c > 0)
    def _():
        for copy in halos:
            copy.wait_recv()

    @pl.when(c == 0)
    def _():
        r.halo_x[...] = jnp.zeros_like(r.halo_x)
        r.halo_c[...] = jnp.zeros_like(r.halo_c)

    r.inner[...] = conv_part(r.x, r.halo_x[...].astype(F32), r.conv, r.pad)
    r.coup[...] = conv_part(r.cpl, r.halo_c[...].astype(F32), r.conv_cpl, r.pad_c)
    states = []
    drops = []
    for b in range(COUNT // SPAN):
        part = slice(b * SPAN, (b + 1) * SPAN)
        cums = r.cums[:, part]
        last = cums[:, SPAN - 1 : SPAN]
        tail = jnp.exp(last - cums) * r.steps[:, part]
        weighted = (r.inner[part, :].astype(F32) * spread_cols(tail, expand)).astype(BF16)
        states.append(
            lax.dot_general(
                r.coup[part, :STATE],
                weighted,
                (((0,), (0,)), ((), ())),
                preferred_element_type=F32,
            )
        )
        drops.append(spread_row(jnp.exp(last), expand))
    r.first[...] = states[0]
    run = drops[1] * states[0] + states[1]
    r.run[...] = run
    r.reach[...] = drops[0] * drops[1]
    r.drop[...] = drops[0]
    r.mine[...] = run.astype(BF16)

    def local_part():
        lane = lax.broadcasted_iota(jnp.int32, (SPAN, 2 * HDIM), 1)
        skip = spread_row(diagonal(r.skip[...]), expand)
        for b in range(COUNT // SPAN):
            part = slice(b * SPAN, (b + 1) * SPAN)
            scores = lax.dot_general(
                r.coup[part, STATE:],
                r.coup[part, :STATE],
                (((1,), (1,)), ((), ())),
                preferred_element_type=F32,
            )
            scores = jnp.where(above, scores, 0.0)
            cums = r.cums[:, part]
            turned = cums.T
            opened = silu(r.gate[part, :].astype(F32))
            r.growth[part, :] = spread_cols(jnp.exp(cums), expand) * opened
            for pair in range(HEADS // 2):
                cols = slice(pair * 2 * HDIM, (pair + 1) * 2 * HDIM)
                values = r.inner[part, cols]
                halves = []
                for h in (2 * pair, 2 * pair + 1):
                    spread = turned[:, h : h + 1] - cums[h : h + 1, :]
                    decay = jnp.exp(jnp.where(above, spread, 0.0))
                    mixing = (scores * decay * r.steps[h : h + 1, part]).astype(BF16)
                    halves.append(jnp.dot(mixing, values, preferred_element_type=F32))
                local = jnp.where(lane < HDIM, halves[0], halves[1])
                mixed = local + skip[:, cols] * values.astype(F32)
                r.gated[part, cols] = mixed * opened[:, cols]

    pairs = [
        remote(r.mine, r.theirs, r.pair_send.at[0], r.pair_recv.at[0], {"ctx": partner}),
        remote(r.reach, r.their_reach, r.pair_send.at[1], r.pair_recv.at[1], {"ctx": partner}),
    ]
    lines = STATE // CHUNKS
    spans = [pl.ds(i * lines, lines) for i in range(CHUNKS)]
    ahead = [
        remote(r.onward.at[s], r.arriving.at[s], r.chain_send.at[i], r.chain_recv.at[i], {"ctx": up})
        for i, s in enumerate(spans)
    ]
    relays = [
        remote(
            r.arriving.at[s],
            r.arriving.at[s],
            r.relay_send.at[i],
            r.chain_recv.at[i],
            {"ctx": partner},
        )
        for i, s in enumerate(spans)
    ]

    @pl.when(core == 0)
    def _():
        for copy in pairs:
            copy.start()

    loads[0].wait()
    early = z >= 3

    @pl.when(early)
    def _():
        local_part()

    @pl.when((core == 0) & (z == 0))
    def _():
        r.entry[...] = jnp.zeros_like(r.entry)

    @pl.when((core == 0) & (z > 0))
    def _():
        for i, s in enumerate(spans):
            relays[i].wait_recv()
            r.entry[s, :] = r.arriving[s, :].astype(F32)

    @pl.when(core == 1)
    def _():
        for copy in pairs:
            copy.wait_recv()

        @pl.when(z == 0)
        def _():
            for i, s in enumerate(spans):
                start = r.theirs[s, :].astype(F32)
                r.onward[s, :] = (r.reach[...] * start + r.run[s, :]).astype(BF16)
                ahead[i].start()
                r.entry[s, :] = start

        @pl.when(z > 0)
        def _():
            for i, s in enumerate(spans):
                start = r.theirs[s, :].astype(F32)
                ahead[i].wait_recv()
                inside = r.their_reach[...] * r.arriving[s, :].astype(F32) + start
                r.onward[s, :] = (r.reach[...] * inside + r.run[s, :]).astype(BF16)

                @pl.when(z < RING - 1)
                def _():
                    ahead[i].start()

                relays[i].start()
                r.entry[s, :] = inside

    @pl.when(hold & (z < 4))
    def _():
        up_late.start()

    @pl.when(hold)
    def _():
        downs_up[0].start()

    @pl.when(jnp.logical_not(early))
    def _():
        local_part()

    ups_down[0].wait_recv()
    ups_down[1].start()

    for b in range(COUNT // SPAN):
        part = slice(b * SPAN, (b + 1) * SPAN)
        entry = r.entry[...]
        if b == 1:
            entry = r.drop[...] * entry + r.first[...]
        carried = jnp.dot(r.coup[part, STATE:], entry.astype(BF16), preferred_element_type=F32)
        gated = r.gated[part, :] + carried * r.growth[part, :]
        r.gated[part, :] = gated
        scaled = (gated * r.norm_gain[...]).astype(BF16)
        r.byx[part, :] = scaled
        for k in range(SPAN // TOK):
            at_x, at_y = divmod(b * (SPAN // TOK) + k, 4)
            r.byy[(at_y * 4 + at_x) * TOK : (at_y * 4 + at_x + 1) * TOK, :] = scaled[
                k * TOK : (k + 1) * TOK, :
            ]

    half = D // 2
    quarter = half // 2
    low = pl.ds(0, quarter)
    high = pl.ds(quarter, quarter)

    def squares_copy(i):
        return remote(
            r.squares, r.all_squares.at[i], r.sq_send.at[i], r.sq_recv.at[i], {"exp": peer(i)}
        )

    def along_x(by):
        return {"exp": lax.rem(x + by, 4) * 4 + y}

    def along_y(by):
        return {"exp": x * 4 + lax.rem(y + by, 4)}

    def message(stage, side, number, src):
        slot = stage * 12 + side * 6 + number
        toward = along_x if side == stage else along_y
        landing = (r.near if stage == 0 else r.far).at[side, number]
        return remote(
            src,
            landing,
            r.ring_send.at[slot],
            r.ring_recv.at[slot],
            toward(1 if number % 2 == 0 else 3),
        )

    def block(stage, side, offset):
        if stage == 0:
            return r.parts.at[side, offset]
        place = y if side == 0 else x
        start = pl.multiple_of(lax.rem(place + offset, 4) * TOK, TOK)
        return r.joined.at[side, pl.ds(start, TOK)]

    def sources(stage, side):
        across = block(stage, side, 2)
        right = block(stage, side, 1)
        left = block(stage, side, 3)
        sums = r.near_sum if stage == 0 else r.far_sum
        return [
            across.at[:, low],
            across.at[:, high],
            right.at[:, high],
            left.at[:, low],
            sums.at[side, 0],
            sums.at[side, 1],
        ]

    copies = [
        [
            [message(stage, side, n, src) for n, src in enumerate(sources(stage, side))]
            for side in range(2)
        ]
        for stage in range(2)
    ]

    def multiply(side, offset):
        rows_ref = r.byx if side == 0 else r.byy
        place = x if side == 0 else y
        start = pl.multiple_of(lax.rem(place + offset, 4) * 128, 128)
        rows = rows_ref[pl.ds(start, 128), :]

        def one(i, carry):
            source = pl.ds(pl.multiple_of(side * half + i * 512, 512), 512)
            target = pl.ds(pl.multiple_of(i * 512, 512), 512)
            r.parts[side, offset, :, target] = jnp.dot(
                rows, r.w[:, source], preferred_element_type=F32
            ).astype(BF16)
            return carry

        lax.fori_loop(0, half // 512, one, 0)

    def pass_on(stage, side):
        landing = r.near if stage == 0 else r.far
        sums = r.near_sum if stage == 0 else r.far_sum
        copies[stage][side][0].wait_recv()
        sums[side, 0] = (
            block(stage, side, 1)[:, low].astype(F32) + landing[side, 0].astype(F32)
        ).astype(BF16)
        copies[stage][side][4].start()
        copies[stage][side][1].wait_recv()
        sums[side, 1] = (
            block(stage, side, 3)[:, high].astype(F32) + landing[side, 1].astype(F32)
        ).astype(BF16)
        copies[stage][side][5].start()

    def collect(stage, side):
        landing = r.near if stage == 0 else r.far
        for n in (2, 3, 4, 5):
            copies[stage][side][n].wait_recv()
        own = block(stage, side, 0)
        first = own[:, low].astype(F32) + landing[side, 4].astype(F32)
        first = first + landing[side, 3].astype(F32)
        second = own[:, high].astype(F32) + landing[side, 2].astype(F32)
        second = second + landing[side, 5].astype(F32)
        return first, second

    loads[1].wait()
    for side in range(2):
        multiply(side, 2)
        copies[0][side][0].start()
        copies[0][side][1].start()
    up_early.wait_recv()
    up_late.wait_recv()
    ups_up[1].start()
    for side in range(2):
        multiply(side, 1)
        copies[0][side][2].start()
        multiply(side, 3)
        copies[0][side][3].start()
    downs_down[0].wait_recv()
    downs_down[1].start()
    for side in range(2):
        pass_on(0, side)
    downs_up[0].wait_recv()
    downs_up[1].start()
    for side in range(2):
        multiply(side, 0)
    gated = r.gated[...]
    r.squares[...] = lax.dot_general(
        jnp.ones((8, WIDTH), F32),
        gated * gated,
        (((1,), (1,)), ((), ())),
        precision=HIGH,
        preferred_element_type=F32,
    )[0:1, :]

    def send_squares(i, carry):
        squares_copy(i).start()
        return carry

    lax.fori_loop(1, FLIGHT, send_squares, 0)
    for side in range(2):
        first, second = collect(0, side)
        r.joined[side, :, low] = first.astype(BF16)
        r.joined[side, :, high] = second.astype(BF16)
        for n in range(4):
            copies[1][side][n].start()
    ups_down[1].wait_recv()
    ups_down[2].start()
    ups_up[1].wait_recv()
    ups_up[2].start()
    for side in range(2):
        pass_on(1, side)
    downs_down[1].wait_recv()
    downs_down[2].start()
    downs_up[1].wait_recv()
    downs_up[2].start()
    for side in range(2):
        first, second = collect(1, side)
        r.owned[:, pl.ds(side * half, quarter)] = first
        r.owned[:, pl.ds(side * half + quarter, quarter)] = second
    r.all_squares[0] = r.squares[...]

    def take_squares(i, carry):
        squares_copy(i).wait()
        return carry

    lax.fori_loop(1, FLIGHT, take_squares, 0)
    total = r.all_squares[0]
    for i in range(1, FLIGHT):
        total = total + r.all_squares[i]

    loads[2].wait()
    loads[3].wait()
    wide_row = lax.broadcasted_iota(jnp.int32, (TOK, COUNT), 0)
    wide_col = lax.broadcasted_iota(jnp.int32, (TOK, COUNT), 1)
    squares = jnp.sum(
        jnp.where(wide_col == me * TOK + wide_row, total, 0.0), axis=1, keepdims=True
    )
    hidden = r.residual[...].astype(F32) + r.owned[...] * lax.rsqrt(squares / INNER + EPS)
    r.hidden[...] = hidden
    mean = jnp.sum(hidden * hidden, axis=1, keepdims=True) / D
    normed = (hidden * lax.rsqrt(mean + EPS) * r.moe_gain[...]).astype(BF16)
    for s in range(2 * RING):
        r.normed[s] = normed[:, s * SLICE : (s + 1) * SLICE]
    expert = lax.broadcasted_iota(jnp.int32, (TOK, NEXP), 1)
    named = expert < 0
    for k in range(TOPK):
        choice = diagonal(r.routes[k : k + 1, :].astype(F32))
        named = named | (choice.astype(jnp.int32) == expert)
    order = r.priority[...].astype(F32)
    earlier = (order < diagonal(order)).astype(F32).astype(BF16)
    rank = jnp.dot(earlier, named.astype(F32).astype(BF16), preferred_element_type=F32)
    key = jnp.where(named, rank, 99.0).astype(BF16)
    lanes = FLIGHT * CAP
    widen_row = lax.broadcasted_iota(jnp.int32, (NEXP, lanes), 0)
    widen_col = lax.broadcasted_iota(jnp.int32, (NEXP, lanes), 1)
    widen = (lax.div(widen_col, CAP) == widen_row).astype(F32).astype(BF16)
    key_wide = jnp.dot(key, widen, preferred_element_type=F32)
    slot = lax.rem(lax.broadcasted_iota(jnp.int32, (TOK, lanes), 1), CAP).astype(F32)
    chosen = (key_wide == slot).astype(F32)
    pick = chosen.astype(BF16)

    def source(n):
        if n <= 3:
            return lax.rem(z + RING - n, RING)
        if n <= 6:
            return lax.rem(z + n - 3, RING)
        return lax.rem(z + 4, RING)

    def row_copy(g, i):
        other, other_core, device = mate(i)
        return remote(
            r.rows.at[g, other_core, other],
            r.landed.at[g, me, core],
            r.row_send.at[g, i],
            r.row_recv.at[g, i],
            device,
        )

    own_rows = []
    for g in range(2):
        for j in range(2):
            for k, n in enumerate(GROUPS[g]):
                taken = lax.dot_general(
                    pick,
                    r.normed[2 * source(n) + j],
                    (((0,), (0,)), ((), ())),
                    preferred_element_type=F32,
                )
                r.rows[g, j, :, :, k * SLICE : (k + 1) * SLICE] = taken.reshape(
                    FLIGHT, CAP, SLICE
                ).astype(BF16)

        def start_rows(i, carry):
            row_copy(g, i).start()
            return carry

        lax.fori_loop(1, PLANE, start_rows, 0)
        own_rows.append(
            pltpu.make_async_copy(
                r.rows.at[g, core, me], r.landed.at[g, me, core], r.own_sem.at[g]
            )
        )
        own_rows[g].start()

    logits = lax.dot_general(
        normed, r.router[...], (((1,), (1,)), ((), ())), preferred_element_type=F32
    )
    raised = jnp.where(named, jnp.exp(logits), 0.0)
    share = (raised / jnp.sum(raised, axis=1, keepdims=True)).astype(BF16)
    share_wide = jnp.dot(share, widen, preferred_element_type=F32)
    r.share[...] = (chosen * share_wide).astype(BF16)
    ups_down[2].wait_recv()
    ups_down[3].start()
    ups_up[2].wait_recv()
    ups_up[3].start()

    loads[4].wait()
    loads[5].wait()
    for g in range(2):
        if g == 1:
            downs_up[2].wait_recv()
            downs_up[3].start()
            downs_down[2].wait_recv()
            downs_down[3].start()
        own_rows[g].wait()

        def take_rows(i, carry):
            row_copy(g, i).wait()
            return carry

        lax.fori_loop(1, PLANE, take_rows, 0)
        for k, n in enumerate(GROUPS[g]):
            cols = slice(k * SLICE, (k + 1) * SLICE)
            r.tokens[n] = (
                r.landed[g, :, :, :, cols].astype(F32).reshape(PLANE * CAP, SLICE).astype(BF16)
            )

        def gate_up(i, carry):
            cols = pl.ds(pl.multiple_of(i * 256, 256), 256)
            total = None if g == 0 else r.units[:, cols]
            for n in GROUPS[g]:
                if n == 7:
                    continue
                value = jnp.dot(r.tokens[n], r.ups[n, :, cols], preferred_element_type=F32)
                total = value if total is None else total + value
            r.units[:, cols] = total
            return carry

        lax.fori_loop(0, 2 * FFE // 256, gate_up, 0)
    ups_up[3].wait_recv()
    ups_down[3].wait_recv()

    def last_slice(i, carry):
        cols = pl.ds(pl.multiple_of(i * 256, 256), 256)
        total = r.units[:, cols] + jnp.dot(
            r.tokens[7], r.ups[7, :, cols], preferred_element_type=F32
        )
        r.units[:, cols] = total
        r.units_out[:, cols] = total.astype(BF16)
        return carry

    lax.fori_loop(0, 2 * FFE // 256, last_slice, 0)
    swap = remote(r.units_out, r.units_in, r.pair_send.at[2], r.pair_recv.at[2], {"ctx": partner})
    swap.start()
    swap.wait()
    gate = r.units[:, :FFE] + r.units_in[:, :FFE].astype(F32)
    lift = r.units[:, FFE:] + r.units_in[:, FFE:].astype(F32)
    activated = (silu(gate) * lift).astype(BF16)

    def back_copy(g, i):
        other, other_core, device = mate(i)
        return remote(
            r.answers.at[g, other, other_core],
            r.back.at[g, me, core],
            r.back_send.at[g, i],
            r.back_recv.at[g, i],
            device,
        )

    own_back = []
    for g in range(2):
        for k, n in enumerate(GROUPS[g]):
            if n == 7:
                downs_up[3].wait_recv()
                downs_down[3].wait_recv()
            values = lax.dot_general(
                activated, r.downs[n], (((1,), (1,)), ((), ())), preferred_element_type=F32
            )
            r.answers[g, :, :, :, k * SLICE : (k + 1) * SLICE] = values.reshape(
                FLIGHT, 2, CAP, SLICE
            ).astype(BF16)

        def start_back(i, carry):
            back_copy(g, i).start()
            return carry

        lax.fori_loop(1, PLANE, start_back, 0)
        own_back.append(
            pltpu.make_async_copy(
                r.answers.at[g, me, core], r.back.at[g, me, core], r.own_sem.at[2 + g]
            )
        )
        own_back[g].start()

    for g in range(2):
        own_back[g].wait()

        def take_back(i, carry):
            back_copy(g, i).wait()
            return carry

        lax.fori_loop(1, PLANE, take_back, 0)
        weights = r.share[...]
        for j in range(2):
            rows = r.back[g, :, j].astype(F32).reshape(FLIGHT * CAP, quarter).astype(BF16)
            total = jnp.dot(weights, rows, preferred_element_type=F32)
            for k, n in enumerate(GROUPS[g]):
                place = pl.multiple_of((2 * source(n) + j) * SLICE, SLICE)
                r.moe_out[:, pl.ds(place, SLICE)] = total[:, k * SLICE : (k + 1) * SLICE]

    @pl.when(c < 2 * RING - 1)
    def _():
        for copy in halos:
            copy.wait_send()

    @pl.when(core == 0)
    def _():
        for copy in pairs:
            copy.wait_send()

    @pl.when(hold)
    def _():
        for copy in ahead:
            copy.wait_send()

    @pl.when((core == 1) & (z > 0))
    def _():
        for copy in relays:
            copy.wait_send()

    for stage in range(2):
        for side in range(2):
            for copy in copies[stage][side]:
                copy.wait_send()
    for copy in [up_early, up_late] + ups_up[1:] + ups_down + downs_up + downs_down:
        copy.wait_send()


def body(
    inner_input,
    gate_input,
    coupling_input,
    step_input,
    conv_inner,
    conv_coupling,
    decay_log,
    skip_gain,
    norm_gain,
    out_weight,
    residual,
    moe_gain,
    router_weight,
    routes,
    priority,
    expert_in,
    expert_out,
):
    return pl.pallas_call(
        layer_kernel,
        out_shape=(shaped((TOK, D), F32), shaped((TOK, D), F32)),
        in_specs=[vmem()] * 11 + [anyspace()] * 6,
        out_specs=(vmem(), vmem()),
        scratch_shapes=list(scratch().values()),
        compiler_params=pltpu.CompilerParams(
            vmem_limit_bytes=VMEM_LIMIT, collective_id=0, has_side_effects=True
        ),
    )(
        inner_input,
        coupling_input,
        step_input.T,
        conv_inner,
        conv_coupling,
        decay_log[None, :],
        skip_gain[None, :],
        norm_gain[None, :],
        moe_gain[None, :],
        routes.T,
        priority,
        gate_input,
        out_weight,
        residual,
        router_weight.T,
        expert_in[0],
        expert_out[0],
    )


def solution(mesh):
    placed = (
        P("ctx", "exp"),
        P("ctx", "exp"),
        P("ctx", None),
        P("ctx", "exp"),
        P(None, "exp"),
        P(),
        P("exp"),
        P("exp"),
        P("exp"),
        P("exp", None),
        P(("ctx", "exp"), None),
        P(),
        P(),
        P(("ctx", "exp"), None),
        P(("ctx", "exp"), None),
        P("exp", "ctx", None),
        P("exp", "ctx", None),
    )
    return jax.shard_map(
        body,
        mesh=mesh,
        in_specs=placed,
        out_specs=(P(("ctx", "exp"), None), P(("ctx", "exp"), None)),
        check_vma=False,
    )
```

```python
from types import SimpleNamespace

import jax
import jax.numpy as jnp
from jax import lax
from jax.experimental import pallas as pl
from jax.experimental.pallas import tpu as pltpu
from jax.sharding import PartitionSpec as P

HDIM = 64
STATE = 128
KCONV = 4
NEXP = 72
TOPK = 10
FFE = 768
SPAN = 256
INNER = 8192
D = 4096
HEADS = 8
WIDTH = 512
COUNT = 512
TOK = 32
CAP = 8
FLIGHT = 16
SLICE = 256
RING = 8
CHUNKS = 8
EDGE = 16
PLANE = 32
GROUPS = ((0, 1, 4, 2), (5, 3, 6, 7))

EPS = 1e-05
HIGH = lax.Precision.HIGHEST
F32 = jnp.float32
BF16 = jnp.bfloat16
MESH = pl.DeviceIdType.MESH
VMEM_LIMIT = 60 * 1024 * 1024


def vmem():
    return pl.BlockSpec(memory_space=pltpu.VMEM)


def anyspace():
    return pl.BlockSpec(memory_space=pl.ANY)


def shaped(shape, dtype):
    return jax.ShapeDtypeStruct(shape, dtype)


def silu(x):
    return x * jax.nn.sigmoid(x)


def where_am_i():
    c = lax.axis_index("ctx")
    e = lax.axis_index("exp")
    return lax.div(c, 2), lax.rem(c, 2), lax.div(e, 4), lax.rem(e, 4)


def up_down(z, core):
    up = lax.rem(z + 1, RING) * 2 + core
    down = lax.rem(z + RING - 1, RING) * 2 + core
    return up, down


def remote(src, dst, send, recv, device):
    return pltpu.make_async_remote_copy(
        src_ref=src,
        dst_ref=dst,
        send_sem=send,
        recv_sem=recv,
        device_id=device,
        device_id_type=MESH,
    )


def conv_part(src_ref, halo, weight_ref, pad_ref):
    count = src_ref.shape[0]
    pad_ref[0:EDGE, :] = halo
    pad_ref[EDGE : EDGE + count, :] = src_ref[...].astype(F32)
    first = EDGE - KCONV + 1
    total = weight_ref[0:1, :] * pad_ref[first : first + count, :]
    for k in range(1, KCONV):
        total = total + weight_ref[k : k + 1, :] * pad_ref[first + k : first + k + count, :]
    return silu(total).astype(BF16)


def expander():
    row = lax.broadcasted_iota(jnp.int32, (HEADS, WIDTH), 0)
    lane = lax.broadcasted_iota(jnp.int32, (HEADS, WIDTH), 1)
    return (lax.div(lane, HDIM) == row).astype(F32)


def spread_cols(values, expand):
    return lax.dot_general(
        values, expand, (((0,), (0,)), ((), ())), precision=HIGH, preferred_element_type=F32
    )


def spread_row(column, expand):
    return jnp.sum(column * expand, axis=0, keepdims=True)


def diagonal(row):
    n = row.shape[1]
    a = lax.broadcasted_iota(jnp.int32, (n, n), 0)
    b = lax.broadcasted_iota(jnp.int32, (n, n), 1)
    return jnp.sum(jnp.where(a == b, row, 0.0), axis=1, keepdims=True)


INPUTS = [
    "x",
    "cpl",
    "step",
    "conv",
    "conv_cpl",
    "decay",
    "skip",
    "norm_gain",
    "moe_gain",
    "routes",
    "priority",
    "gate_in",
    "out_w",
    "residual_in",
    "router_in",
    "wi",
    "wo",
]
OUTPUTS = ["hidden", "moe_out"]


def scratch():
    dma = pltpu.SemaphoreType.DMA
    V = pltpu.VMEM
    half, quarter = D // 2, D // 4
    return {
        "gate": V((COUNT, WIDTH), BF16),
        "w": V((WIDTH, D), BF16),
        "residual": V((TOK, D), BF16),
        "router": V((NEXP, D), BF16),
        "halo_x": V((EDGE, WIDTH), BF16),
        "halo_c": V((EDGE, 2 * STATE), BF16),
        "pad": V((COUNT + EDGE, WIDTH), F32),
        "pad_c": V((COUNT + EDGE, 2 * STATE), F32),
        "inner": V((COUNT, WIDTH), BF16),
        "coup": V((COUNT, 2 * STATE), BF16),
        "steps": V((HEADS, COUNT), F32),
        "cums": V((HEADS, COUNT), F32),
        "first": V((STATE, WIDTH), F32),
        "run": V((STATE, WIDTH), F32),
        "reach": V((1, WIDTH), F32),
        "drop": V((1, WIDTH), F32),
        "entry": V((STATE, WIDTH), F32),
        "gated": V((COUNT, WIDTH), F32),
        "growth": V((COUNT, WIDTH), F32),
        "byx": V((COUNT, WIDTH), BF16),
        "byy": V((COUNT, WIDTH), BF16),
        "squares": V((1, COUNT), F32),
        "sums": V((1, COUNT), F32),
        "mine": V((STATE, WIDTH), BF16),
        "theirs": V((STATE, WIDTH), BF16),
        "their_reach": V((1, WIDTH), F32),
        "arriving": V((STATE, WIDTH), BF16),
        "onward": V((STATE, WIDTH), BF16),
        "parts": V((2, 4, 128, half), BF16),
        "near": V((2, 6, 128, quarter), BF16),
        "far": V((2, 6, TOK, quarter), BF16),
        "joined": V((2, 128, half), BF16),
        "near_sum": V((2, 2, 128, quarter), BF16),
        "far_sum": V((2, 2, TOK, quarter), BF16),
        "all_squares": V((FLIGHT, 1, COUNT), F32),
        "owned": V((TOK, D), F32),
        "normed": V((2 * RING, TOK, SLICE), BF16),
        "share": V((TOK, FLIGHT * CAP), BF16),
        "rows": V((2, 2, FLIGHT, CAP, quarter), BF16),
        "landed": V((2, FLIGHT, 2, CAP, quarter), BF16),
        "tokens": V((RING, PLANE * CAP, SLICE), BF16),
        "ups": V((RING, SLICE, 2 * FFE), BF16),
        "downs": V((RING, SLICE, FFE), BF16),
        "units": V((PLANE * CAP, 2 * FFE), F32),
        "units_out": V((PLANE * CAP, 2 * FFE), BF16),
        "units_in": V((PLANE * CAP, 2 * FFE), BF16),
        "answers": V((2, FLIGHT, 2, CAP, quarter), BF16),
        "back": V((2, FLIGHT, 2, CAP, quarter), BF16),
        "load_sem": dma((6,)),
        "halo_send": dma((2,)),
        "halo_recv": dma((2,)),
        "pair_send": dma((8,)),
        "pair_recv": dma((8,)),
        "chain_send": dma((CHUNKS,)),
        "chain_recv": dma((CHUNKS,)),
        "relay_send": dma((CHUNKS,)),
        "hop_send": dma((17,)),
        "hop_recv": dma((17,)),
        "ring_send": dma((24,)),
        "ring_recv": dma((24,)),
        "sq_send": dma((FLIGHT,)),
        "sq_recv": dma((FLIGHT,)),
        "row_send": dma((2, PLANE)),
        "row_recv": dma((2, PLANE)),
        "back_send": dma((2, PLANE)),
        "back_recv": dma((2, PLANE)),
        "own_sem": dma((4,)),
    }


def layer_kernel(*refs):
    r = SimpleNamespace(**dict(zip(INPUTS + OUTPUTS + list(scratch()), refs, strict=True)))
    z, core, x, y = where_am_i()
    c = z * 2 + core
    me = x * 4 + y
    up, down = up_down(z, core)
    partner = z * 2 + 1 - core
    after = lax.rem(c + 1, 2 * RING)
    before = lax.rem(c + 2 * RING - 1, 2 * RING)
    cross = jnp.where(core == 0, before, after)

    def peer(i):
        return lax.rem(me + i, FLIGHT)

    def mate(i):
        other = lax.rem(me + lax.div(i, 2), FLIGHT)
        other_core = lax.rem(core + i, 2)
        return other, other_core, {"ctx": z * 2 + other_core, "exp": other}

    barrier = pltpu.get_barrier_semaphore()
    for other in (up, down, cross):
        pl.semaphore_signal(barrier, inc=1, device_id={"ctx": other}, device_id_type=MESH)

    def greet(i, carry):
        pl.semaphore_signal(barrier, inc=1, device_id=mate(i)[2], device_id_type=MESH)
        return carry

    lax.fori_loop(1, PLANE, greet, 0)
    loads = [
        pltpu.make_async_copy(src, dst, r.load_sem.at[i])
        for i, (src, dst) in enumerate(
            (
                (r.gate_in, r.gate),
                (r.out_w, r.w),
                (r.residual_in, r.residual),
                (r.router_in, r.router),
                (r.wi, r.ups.at[0]),
                (r.wo, r.downs.at[0]),
            )
        )
    ]
    for copy in loads:
        copy.start()

    raw = r.step[...]
    steps = jnp.maximum(raw, 0.0) + jnp.log1p(jnp.exp(-jnp.abs(raw)))
    r.steps[...] = steps
    rate = steps * (-jnp.exp(diagonal(r.decay[...])))
    pl.semaphore_wait(barrier, PLANE + 2)

    halos = [
        remote(
            r.x.at[pl.ds(COUNT - EDGE, EDGE)],
            r.halo_x,
            r.halo_send.at[0],
            r.halo_recv.at[0],
            {"ctx": after},
        ),
        remote(
            r.cpl.at[pl.ds(COUNT - EDGE, EDGE)],
            r.halo_c,
            r.halo_send.at[1],
            r.halo_recv.at[1],
            {"ctx": after},
        ),
    ]

    def hop(slot, src, dst, toward):
        return remote(src, dst, r.hop_send.at[slot], r.hop_recv.at[slot], {"ctx": toward})

    cut = SLICE // 2
    low_rows, high_rows = pl.ds(0, cut), pl.ds(cut, cut)
    up_early = hop(0, r.wi.at[low_rows], r.ups.at[1, low_rows], up)
    up_late = hop(1, r.wi.at[high_rows], r.ups.at[1, high_rows], up)
    ups_up = [None]
    ups_down = [hop(2, r.wi, r.ups.at[4], down)]
    downs_up = [hop(3, r.wo, r.downs.at[1], up)]
    downs_down = [hop(4, r.wo, r.downs.at[4], down)]
    for n in (1, 2):
        base = 4 * n + 1
        ups_up.append(hop(base, r.ups.at[n], r.ups.at[n + 1], up))
        ups_down.append(hop(base + 1, r.ups.at[n + 3], r.ups.at[n + 4], down))
        downs_up.append(hop(base + 2, r.downs.at[n], r.downs.at[n + 1], up))
        downs_down.append(hop(base + 3, r.downs.at[n + 3], r.downs.at[n + 4], down))
    ups_up.append(hop(13, r.ups.at[3, low_rows], r.ups.at[7, low_rows], up))
    ups_down.append(hop(14, r.ups.at[6, high_rows], r.ups.at[7, high_rows], down))
    downs_up.append(hop(15, r.downs.at[3, low_rows], r.downs.at[7, low_rows], up))
    downs_down.append(hop(16, r.downs.at[6, high_rows], r.downs.at[7, high_rows], down))

    @pl.when(c < 2 * RING - 1)
    def _():
        for copy in halos:
            copy.start()

    hold = (core == 1) & (z < RING - 1)
    up_early.start()
    ups_down[0].start()
    downs_down[0].start()

    @pl.when(jnp.logical_not(hold) | (z >= 4))
    def _():
        up_late.start()

    @pl.when(jnp.logical_not(hold))
    def _():
        downs_up[0].start()

    row = lax.broadcasted_iota(jnp.int32, (SPAN, SPAN), 0)
    col = lax.broadcasted_iota(jnp.int32, (SPAN, SPAN), 1)
    upper = (row <= col).astype(F32)
    above = row >= col
    expand = expander()
    for b in range(COUNT // SPAN):
        part = slice(b * SPAN, (b + 1) * SPAN)
        r.cums[:, part] = jnp.dot(
            rate[:, part], upper, precision=HIGH, preferred_element_type=F32
        )

    @pl.when(c > 0)
    def _():
        for copy in halos:
            copy.wait_recv()

    @pl.when(c == 0)
    def _():
        r.halo_x[...] = jnp.zeros_like(r.halo_x)
        r.halo_c[...] = jnp.zeros_like(r.halo_c)

    r.inner[...] = conv_part(r.x, r.halo_x[...].astype(F32), r.conv, r.pad)
    r.coup[...] = conv_part(r.cpl, r.halo_c[...].astype(F32), r.conv_cpl, r.pad_c)
    states = []
    drops = []
    for b in range(COUNT // SPAN):
        part = slice(b * SPAN, (b + 1) * SPAN)
        cums = r.cums[:, part]
        last = cums[:, SPAN - 1 : SPAN]
        tail = jnp.exp(last - cums) * r.steps[:, part]
        weighted = (r.inner[part, :].astype(F32) * spread_cols(tail, expand)).astype(BF16)
        states.append(
            lax.dot_general(
                r.coup[part, :STATE],
                weighted,
                (((0,), (0,)), ((), ())),
                preferred_element_type=F32,
            )
        )
        drops.append(spread_row(jnp.exp(last), expand))
    r.first[...] = states[0]
    run = drops[1] * states[0] + states[1]
    r.run[...] = run
    r.reach[...] = drops[0] * drops[1]
    r.drop[...] = drops[0]
    r.mine[...] = run.astype(BF16)

    def local_part():
        lane = lax.broadcasted_iota(jnp.int32, (SPAN, 2 * HDIM), 1)
        skip = spread_row(diagonal(r.skip[...]), expand)
        for b in range(COUNT // SPAN):
            part = slice(b * SPAN, (b + 1) * SPAN)
            scores = lax.dot_general(
                r.coup[part, STATE:],
                r.coup[part, :STATE],
                (((1,), (1,)), ((), ())),
                preferred_element_type=F32,
            )
            scores = jnp.where(above, scores, 0.0)
            cums = r.cums[:, part]
            turned = cums.T
            opened = silu(r.gate[part, :].astype(F32))
            r.growth[part, :] = spread_cols(jnp.exp(cums), expand) * opened
            for pair in range(HEADS // 2):
                cols = slice(pair * 2 * HDIM, (pair + 1) * 2 * HDIM)
                values = r.inner[part, cols]
                halves = []
                for h in (2 * pair, 2 * pair + 1):
                    spread = turned[:, h : h + 1] - cums[h : h + 1, :]
                    decay = jnp.exp(jnp.where(above, spread, 0.0))
                    mixing = (scores * decay * r.steps[h : h + 1, part]).astype(BF16)
                    halves.append(jnp.dot(mixing, values, preferred_element_type=F32))
                local = jnp.where(lane < HDIM, halves[0], halves[1])
                mixed = local + skip[:, cols] * values.astype(F32)
                r.gated[part, cols] = mixed * opened[:, cols]

    pairs = [
        remote(r.mine, r.theirs, r.pair_send.at[0], r.pair_recv.at[0], {"ctx": partner}),
        remote(r.reach, r.their_reach, r.pair_send.at[1], r.pair_recv.at[1], {"ctx": partner}),
    ]
    lines = STATE // CHUNKS
    spans = [pl.ds(i * lines, lines) for i in range(CHUNKS)]
    ahead = [
        remote(r.onward.at[s], r.arriving.at[s], r.chain_send.at[i], r.chain_recv.at[i], {"ctx": up})
        for i, s in enumerate(spans)
    ]
    relays = [
        remote(
            r.arriving.at[s],
            r.arriving.at[s],
            r.relay_send.at[i],
            r.chain_recv.at[i],
            {"ctx": partner},
        )
        for i, s in enumerate(spans)
    ]

    @pl.when(core == 0)
    def _():
        for copy in pairs:
            copy.start()

    loads[0].wait()
    early = z >= 3

    @pl.when(early)
    def _():
        local_part()

    @pl.when((core == 0) & (z == 0))
    def _():
        r.entry[...] = jnp.zeros_like(r.entry)

    @pl.when((core == 0) & (z > 0))
    def _():
        for i, s in enumerate(spans):
            relays[i].wait_recv()
            r.entry[s, :] = r.arriving[s, :].astype(F32)

    @pl.when(core == 1)
    def _():
        for copy in pairs:
            copy.wait_recv()

        @pl.when(z == 0)
        def _():
            for i, s in enumerate(spans):
                start = r.theirs[s, :].astype(F32)
                r.onward[s, :] = (r.reach[...] * start + r.run[s, :]).astype(BF16)
                ahead[i].start()
                r.entry[s, :] = start

        @pl.when(z > 0)
        def _():
            for i, s in enumerate(spans):
                start = r.theirs[s, :].astype(F32)
                ahead[i].wait_recv()
                inside = r.their_reach[...] * r.arriving[s, :].astype(F32) + start
                r.onward[s, :] = (r.reach[...] * inside + r.run[s, :]).astype(BF16)

                @pl.when(z < RING - 1)
                def _():
                    ahead[i].start()

                relays[i].start()
                r.entry[s, :] = inside

    @pl.when(hold & (z < 4))
    def _():
        up_late.start()

    @pl.when(hold)
    def _():
        downs_up[0].start()

    @pl.when(jnp.logical_not(early))
    def _():
        local_part()

    ups_down[0].wait_recv()
    ups_down[1].start()

    for b in range(COUNT // SPAN):
        part = slice(b * SPAN, (b + 1) * SPAN)
        entry = r.entry[...]
        if b == 1:
            entry = r.drop[...] * entry + r.first[...]
        carried = jnp.dot(r.coup[part, STATE:], entry.astype(BF16), preferred_element_type=F32)
        gated = r.gated[part, :] + carried * r.growth[part, :]
        r.gated[part, :] = gated
        scaled = (gated * r.norm_gain[...]).astype(BF16)
        r.byx[part, :] = scaled
        for k in range(SPAN // TOK):
            at_x, at_y = divmod(b * (SPAN // TOK) + k, 4)
            r.byy[(at_y * 4 + at_x) * TOK : (at_y * 4 + at_x + 1) * TOK, :] = scaled[
                k * TOK : (k + 1) * TOK, :
            ]

    half = D // 2
    quarter = half // 2
    low = pl.ds(0, quarter)
    high = pl.ds(quarter, quarter)

    def squares_copy(i):
        return remote(
            r.squares, r.all_squares.at[i], r.sq_send.at[i], r.sq_recv.at[i], {"exp": peer(i)}
        )

    def along_x(by):
        return {"exp": lax.rem(x + by, 4) * 4 + y}

    def along_y(by):
        return {"exp": x * 4 + lax.rem(y + by, 4)}

    def message(stage, side, number, src):
        slot = stage * 12 + side * 6 + number
        toward = along_x if side == stage else along_y
        landing = (r.near if stage == 0 else r.far).at[side, number]
        return remote(
            src,
            landing,
            r.ring_send.at[slot],
            r.ring_recv.at[slot],
            toward(1 if number % 2 == 0 else 3),
        )

    def block(stage, side, offset):
        if stage == 0:
            return r.parts.at[side, offset]
        place = y if side == 0 else x
        start = pl.multiple_of(lax.rem(place + offset, 4) * TOK, TOK)
        return r.joined.at[side, pl.ds(start, TOK)]

    def sources(stage, side):
        across = block(stage, side, 2)
        right = block(stage, side, 1)
        left = block(stage, side, 3)
        sums = r.near_sum if stage == 0 else r.far_sum
        return [
            across.at[:, low],
            across.at[:, high],
            right.at[:, high],
            left.at[:, low],
            sums.at[side, 0],
            sums.at[side, 1],
        ]

    copies = [
        [
            [message(stage, side, n, src) for n, src in enumerate(sources(stage, side))]
            for side in range(2)
        ]
        for stage in range(2)
    ]

    def multiply(side, offset):
        rows_ref = r.byx if side == 0 else r.byy
        place = x if side == 0 else y
        start = pl.multiple_of(lax.rem(place + offset, 4) * 128, 128)
        rows = rows_ref[pl.ds(start, 128), :]

        def one(i, carry):
            source = pl.ds(pl.multiple_of(side * half + i * 512, 512), 512)
            target = pl.ds(pl.multiple_of(i * 512, 512), 512)
            r.parts[side, offset, :, target] = jnp.dot(
                rows, r.w[:, source], preferred_element_type=F32
            ).astype(BF16)
            return carry

        lax.fori_loop(0, half // 512, one, 0)

    def pass_on(stage, side):
        landing = r.near if stage == 0 else r.far
        sums = r.near_sum if stage == 0 else r.far_sum
        copies[stage][side][0].wait_recv()
        sums[side, 0] = (
            block(stage, side, 1)[:, low].astype(F32) + landing[side, 0].astype(F32)
        ).astype(BF16)
        copies[stage][side][4].start()
        copies[stage][side][1].wait_recv()
        sums[side, 1] = (
            block(stage, side, 3)[:, high].astype(F32) + landing[side, 1].astype(F32)
        ).astype(BF16)
        copies[stage][side][5].start()

    def collect(stage, side):
        landing = r.near if stage == 0 else r.far
        for n in (2, 3, 4, 5):
            copies[stage][side][n].wait_recv()
        own = block(stage, side, 0)
        first = own[:, low].astype(F32) + landing[side, 4].astype(F32)
        first = first + landing[side, 3].astype(F32)
        second = own[:, high].astype(F32) + landing[side, 2].astype(F32)
        second = second + landing[side, 5].astype(F32)
        return first, second

    loads[1].wait()
    for side in range(2):
        multiply(side, 2)
        copies[0][side][0].start()
        copies[0][side][1].start()
    up_early.wait_recv()
    up_late.wait_recv()
    ups_up[1].start()
    for side in range(2):
        multiply(side, 1)
        copies[0][side][2].start()
        multiply(side, 3)
        copies[0][side][3].start()
    downs_down[0].wait_recv()
    downs_down[1].start()
    for side in range(2):
        pass_on(0, side)
    downs_up[0].wait_recv()
    downs_up[1].start()
    for side in range(2):
        multiply(side, 0)
    gated = r.gated[...]
    r.squares[...] = lax.dot_general(
        jnp.ones((8, WIDTH), F32),
        gated * gated,
        (((1,), (1,)), ((), ())),
        precision=HIGH,
        preferred_element_type=F32,
    )[0:1, :]

    def send_squares(i, carry):
        squares_copy(i).start()
        return carry

    lax.fori_loop(1, FLIGHT, send_squares, 0)
    for side in range(2):
        first, second = collect(0, side)
        r.joined[side, :, low] = first.astype(BF16)
        r.joined[side, :, high] = second.astype(BF16)
        for n in range(4):
            copies[1][side][n].start()
    ups_down[1].wait_recv()
    ups_down[2].start()
    ups_up[1].wait_recv()
    ups_up[2].start()
    for side in range(2):
        pass_on(1, side)
    downs_down[1].wait_recv()
    downs_down[2].start()
    downs_up[1].wait_recv()
    downs_up[2].start()
    for side in range(2):
        first, second = collect(1, side)
        r.owned[:, pl.ds(side * half, quarter)] = first
        r.owned[:, pl.ds(side * half + quarter, quarter)] = second
    r.all_squares[0] = r.squares[...]

    def take_squares(i, carry):
        squares_copy(i).wait()
        return carry

    lax.fori_loop(1, FLIGHT, take_squares, 0)
    total = r.all_squares[0]
    for i in range(1, FLIGHT):
        total = total + r.all_squares[i]

    loads[2].wait()
    loads[3].wait()
    wide_row = lax.broadcasted_iota(jnp.int32, (TOK, COUNT), 0)
    wide_col = lax.broadcasted_iota(jnp.int32, (TOK, COUNT), 1)
    squares = jnp.sum(
        jnp.where(wide_col == me * TOK + wide_row, total, 0.0), axis=1, keepdims=True
    )
    hidden = r.residual[...].astype(F32) + r.owned[...] * lax.rsqrt(squares / INNER + EPS)
    r.hidden[...] = hidden
    mean = jnp.sum(hidden * hidden, axis=1, keepdims=True) / D
    normed = (hidden * lax.rsqrt(mean + EPS) * r.moe_gain[...]).astype(BF16)
    for s in range(2 * RING):
        r.normed[s] = normed[:, s * SLICE : (s + 1) * SLICE]
    expert = lax.broadcasted_iota(jnp.int32, (TOK, NEXP), 1)
    named = expert < 0
    for k in range(TOPK):
        choice = diagonal(r.routes[k : k + 1, :].astype(F32))
        named = named | (choice.astype(jnp.int32) == expert)
    order = r.priority[...].astype(F32)
    earlier = (order < diagonal(order)).astype(F32).astype(BF16)
    rank = jnp.dot(earlier, named.astype(F32).astype(BF16), preferred_element_type=F32)
    key = jnp.where(named, rank, 99.0).astype(BF16)
    lanes = FLIGHT * CAP
    widen_row = lax.broadcasted_iota(jnp.int32, (NEXP, lanes), 0)
    widen_col = lax.broadcasted_iota(jnp.int32, (NEXP, lanes), 1)
    widen = (lax.div(widen_col, CAP) == widen_row).astype(F32).astype(BF16)
    key_wide = jnp.dot(key, widen, preferred_element_type=F32)
    slot = lax.rem(lax.broadcasted_iota(jnp.int32, (TOK, lanes), 1), CAP).astype(F32)
    chosen = (key_wide == slot).astype(F32)
    pick = chosen.astype(BF16)

    def source(n):
        if n <= 3:
            return lax.rem(z + RING - n, RING)
        if n <= 6:
            return lax.rem(z + n - 3, RING)
        return lax.rem(z + 4, RING)

    def row_copy(g, i):
        other, other_core, device = mate(i)
        return remote(
            r.rows.at[g, other_core, other],
            r.landed.at[g, me, core],
            r.row_send.at[g, i],
            r.row_recv.at[g, i],
            device,
        )

    own_rows = []
    for g in range(2):
        for j in range(2):
            for k, n in enumerate(GROUPS[g]):
                taken = lax.dot_general(
                    pick,
                    r.normed[2 * source(n) + j],
                    (((0,), (0,)), ((), ())),
                    preferred_element_type=F32,
                )
                r.rows[g, j, :, :, k * SLICE : (k + 1) * SLICE] = taken.reshape(
                    FLIGHT, CAP, SLICE
                ).astype(BF16)

        def start_rows(i, carry):
            row_copy(g, i).start()
            return carry

        lax.fori_loop(1, PLANE, start_rows, 0)
        own_rows.append(
            pltpu.make_async_copy(
                r.rows.at[g, core, me], r.landed.at[g, me, core], r.own_sem.at[g]
            )
        )
        own_rows[g].start()

    logits = lax.dot_general(
        normed, r.router[...], (((1,), (1,)), ((), ())), preferred_element_type=F32
    )
    raised = jnp.where(named, jnp.exp(logits), 0.0)
    share = (raised / jnp.sum(raised, axis=1, keepdims=True)).astype(BF16)
    share_wide = jnp.dot(share, widen, preferred_element_type=F32)
    r.share[...] = (chosen * share_wide).astype(BF16)
    ups_down[2].wait_recv()
    ups_down[3].start()
    ups_up[2].wait_recv()
    ups_up[3].start()

    loads[4].wait()
    loads[5].wait()
    for g in range(2):
        if g == 1:
            downs_up[2].wait_recv()
            downs_up[3].start()
            downs_down[2].wait_recv()
            downs_down[3].start()
        own_rows[g].wait()

        def take_rows(i, carry):
            row_copy(g, i).wait()
            return carry

        lax.fori_loop(1, PLANE, take_rows, 0)
        for k, n in enumerate(GROUPS[g]):
            cols = slice(k * SLICE, (k + 1) * SLICE)
            r.tokens[n] = (
                r.landed[g, :, :, :, cols].astype(F32).reshape(PLANE * CAP, SLICE).astype(BF16)
            )

        def gate_up(i, carry):
            cols = pl.ds(pl.multiple_of(i * 256, 256), 256)
            total = None if g == 0 else r.units[:, cols]
            for n in GROUPS[g]:
                if n == 7:
                    continue
                value = jnp.dot(r.tokens[n], r.ups[n, :, cols], preferred_element_type=F32)
                total = value if total is None else total + value
            r.units[:, cols] = total
            return carry

        lax.fori_loop(0, 2 * FFE // 256, gate_up, 0)
    ups_up[3].wait_recv()
    ups_down[3].wait_recv()

    swaps = []
    blocks = [(pl.ds(i, 256), pl.ds(FFE + i, 256)) for i in range(0, FFE, 256)]
    for cols in sum(blocks, ()):
        total = r.units[:, cols] + jnp.dot(
            r.tokens[7], r.ups[7, :, cols], preferred_element_type=F32
        )
        r.units[:, cols] = total
        r.units_out[:, cols] = total.astype(BF16)
        slot = 2 + len(swaps)
        swaps.append(
            remote(
                r.units_out.at[:, cols],
                r.units_in.at[:, cols],
                r.pair_send.at[slot],
                r.pair_recv.at[slot],
                {"ctx": partner},
            )
        )
        swaps[-1].start()
    pieces = []
    for i, (gate_cols, lift_cols) in enumerate(blocks):
        swaps[2 * i].wait_recv()
        gate = r.units[:, gate_cols] + r.units_in[:, gate_cols].astype(F32)
        swaps[2 * i + 1].wait_recv()
        lift = r.units[:, lift_cols] + r.units_in[:, lift_cols].astype(F32)
        pieces.append((silu(gate) * lift).astype(BF16))
    activated = jnp.concatenate(pieces, axis=1)

    def back_copy(g, i):
        other, other_core, device = mate(i)
        return remote(
            r.answers.at[g, other, other_core],
            r.back.at[g, me, core],
            r.back_send.at[g, i],
            r.back_recv.at[g, i],
            device,
        )

    own_back = []
    for g in range(2):
        for k, n in enumerate(GROUPS[g]):
            if n == 7:
                downs_up[3].wait_recv()
                downs_down[3].wait_recv()
            values = lax.dot_general(
                activated, r.downs[n], (((1,), (1,)), ((), ())), preferred_element_type=F32
            )
            r.answers[g, :, :, :, k * SLICE : (k + 1) * SLICE] = values.reshape(
                FLIGHT, 2, CAP, SLICE
            ).astype(BF16)

        def start_back(i, carry):
            back_copy(g, i).start()
            return carry

        lax.fori_loop(1, PLANE, start_back, 0)
        own_back.append(
            pltpu.make_async_copy(
                r.answers.at[g, me, core], r.back.at[g, me, core], r.own_sem.at[2 + g]
            )
        )
        own_back[g].start()

    for g in range(2):
        own_back[g].wait()

        def take_back(i, carry):
            back_copy(g, i).wait()
            return carry

        lax.fori_loop(1, PLANE, take_back, 0)
        weights = r.share[...]
        for j in range(2):
            rows = r.back[g, :, j].astype(F32).reshape(FLIGHT * CAP, quarter).astype(BF16)
            total = jnp.dot(weights, rows, preferred_element_type=F32)
            for k, n in enumerate(GROUPS[g]):
                place = pl.multiple_of((2 * source(n) + j) * SLICE, SLICE)
                r.moe_out[:, pl.ds(place, SLICE)] = total[:, k * SLICE : (k + 1) * SLICE]

    @pl.when(c < 2 * RING - 1)
    def _():
        for copy in halos:
            copy.wait_send()

    @pl.when(core == 0)
    def _():
        for copy in pairs:
            copy.wait_send()

    @pl.when(hold)
    def _():
        for copy in ahead:
            copy.wait_send()

    @pl.when((core == 1) & (z > 0))
    def _():
        for copy in relays:
            copy.wait_send()

    for stage in range(2):
        for side in range(2):
            for copy in copies[stage][side]:
                copy.wait_send()
    for copy in swaps + [up_early, up_late] + ups_up[1:] + ups_down + downs_up + downs_down:
        copy.wait_send()


def body(
    inner_input,
    gate_input,
    coupling_input,
    step_input,
    conv_inner,
    conv_coupling,
    decay_log,
    skip_gain,
    norm_gain,
    out_weight,
    residual,
    moe_gain,
    router_weight,
    routes,
    priority,
    expert_in,
    expert_out,
):
    return pl.pallas_call(
        layer_kernel,
        out_shape=(shaped((TOK, D), F32), shaped((TOK, D), F32)),
        in_specs=[vmem()] * 11 + [anyspace()] * 6,
        out_specs=(vmem(), vmem()),
        scratch_shapes=list(scratch().values()),
        compiler_params=pltpu.CompilerParams(
            vmem_limit_bytes=VMEM_LIMIT, collective_id=0, has_side_effects=True
        ),
    )(
        inner_input,
        coupling_input,
        step_input.T,
        conv_inner,
        conv_coupling,
        decay_log[None, :],
        skip_gain[None, :],
        norm_gain[None, :],
        moe_gain[None, :],
        routes.T,
        priority,
        gate_input,
        out_weight,
        residual,
        router_weight.T,
        expert_in[0],
        expert_out[0],
    )


def solution(mesh):
    placed = (
        P("ctx", "exp"),
        P("ctx", "exp"),
        P("ctx", None),
        P("ctx", "exp"),
        P(None, "exp"),
        P(),
        P("exp"),
        P("exp"),
        P("exp"),
        P("exp", None),
        P(("ctx", "exp"), None),
        P(),
        P(),
        P(("ctx", "exp"), None),
        P(("ctx", "exp"), None),
        P("exp", "ctx", None),
        P("exp", "ctx", None),
    )
    return jax.shard_map(
        body,
        mesh=mesh,
        in_specs=placed,
        out_specs=(P(("ctx", "exp"), None), P(("ctx", "exp"), None)),
        check_vma=False,
    )
```
